32 devices in a mesh: grp: 2 (over x), row: 8 (over z, y), col: 2 (over core).
Axes of the slice: x: 2, y: 2, z: 4, core: 2. Of those that a mesh axis runs over, the one named last changes fastest.
Arguments:
- tokens: int32 [1024, 256], P(('grp', 'row', 'col')), parts along dimension 0, may hold values from 0 to 20
- gap_mask: int32 [1024, 256], P(('grp', 'row', 'col')), parts along dimension 0, may hold values 0 or 1
- dilations: int32 [4], replicated, may hold values from 1 to 4, as said below
- embedding: float32 [21, 64], replicated, may hold values from -6 to 6
- residue_filters: float32 [2, 3, 64, 64], replicated, may hold values from -0.4375 to 0.4375
- projection: bfloat16 [4096, 128], replicated, may hold values from -0.09375 to 0.09375
- pair_filters: bfloat16 [2, 3, 3, 128, 128], replicated, may hold values from -0.1875 to 0.1875
Outputs:
- pair_map: bfloat16 [512, 256, 128], P(('grp', 'row'), 'col'), parts along dimension 0
The draws below stay inside these ranges and needn't reach their ends.
There are 2 independent parts, one for each index of `grp`. The reference program is written for one: setup_inputs(seed, part) draws one part's arguments, and reference() takes and returns one part's arrays. A program takes and returns all parts, laid end to end along the dimension named above; an argument that names none is the same for every part. Nothing has to cross between parts.
Inputs may be any that keep to these rules, and one draw needn't show every extreme that they name: `dilations`: at least one layer has dilation 4.
All inputs are finite; a program needn't handle non-finite values. No bound on the sum of `gap_mask` on one device may be relied on, other than what follows from the above.
Results may differ from the reference program's by a relative error of at most 0.0066.
Values may be sent and summed in bfloat16 or wider, within the bound.
No kernel may reach another device: no remote copies, remote signals or barrier semaphores. Data moves between devices by JAX's collectives and lax.ppermute only.
A program may use at most 128 MiB of HBM per device.

```python
import jax
import jax.numpy as jnp
from jax import lax

NSEQ = 512
L = 256
C = 64
CO = 128
NTOK = 21
NL1 = 2
DMAX = 4


def draw_dilations(key, part):
    layers_all = NL1 + 2
    values = jax.random.randint(jax.random.fold_in(key, 11), (layers_all,), 1, DMAX + 1)
    chosen = jax.random.randint(jax.random.fold_in(key, 12), (), 0, layers_all)
    return jnp.where(jnp.arange(layers_all) == chosen, DMAX, values).astype(jnp.int32)


def touch_ends(values, key, smallest, high):
    index_at = [jax.random.randint(jax.random.fold_in(key, axis), (), 0, length) for axis, length in enumerate(values.shape)]
    main_axis = values.shape.index(max(values.shape))
    next_to = index_at[:main_axis] + [(index_at[main_axis] + 1) % values.shape[main_axis]] + index_at[main_axis + 1:]
    return values.at[tuple(index_at)].set(smallest).at[tuple(next_to)].set(high)


def centred(key, shape, width, limit, kind=jnp.bfloat16):
    return jnp.clip(width * jax.random.normal(key, shape, jnp.float32), -limit, limit).astype(kind)


def setup_inputs(seed: int = 0, part: int = 0) -> dict:
    seeds = jax.random.split(jax.random.key(seed), 8)
    part_splits = jax.random.split(jax.random.fold_in(seeds[7], part), 8)
    return {
        "tokens": touch_ends(jax.random.randint(part_splits[0], (NSEQ, L), 0, NTOK), jax.random.fold_in(part_splits[0], 1), 0, NTOK - 1).astype(jnp.int32),
        "gap_mask": touch_ends((jax.random.randint(part_splits[1], (NSEQ, L), 0, 5) < 4).astype(jnp.int32), jax.random.fold_in(part_splits[1], 1), 0, 1),
        "dilations": draw_dilations(jax.random.fold_in(seeds[7], 71), part),
        "embedding": centred(seeds[3], (NTOK, C), 1.0, 6.0, jnp.float32),
        "residue_filters": centred(seeds[4], (NL1, 3, C, C), (3 * C) ** -0.5, 0.4375, jnp.float32),
        "projection": centred(seeds[5], (C * C, CO), (C * C) ** -0.5, 0.09375),
        "pair_filters": centred(seeds[6], (2, 3, 3, CO, CO), (9 * CO) ** -0.5, 0.1875),
    }


def residue_stack(tokens, gap_mask, dilations, embedding, residue_filters):
    letters = jnp.arange(embedding.shape[0], dtype=jnp.int32)
    onehot = (tokens[:, None, :] == letters[None, :, None]).astype(jnp.float32)
    hidden = jnp.einsum("tc,stl->scl", embedding, onehot, precision=lax.Precision.HIGHEST)
    length = hidden.shape[2]
    for layer_index in range(residue_filters.shape[0]):
        spread = dilations[layer_index]
        padded = jnp.pad(hidden, ((0, 0), (0, 0), (DMAX, DMAX)))
        earlier = lax.dynamic_slice_in_dim(padded, (DMAX - spread).astype(jnp.int32), length, 2)
        latter = lax.dynamic_slice_in_dim(padded, (DMAX + spread).astype(jnp.int32), length, 2)
        mixing = jnp.einsum("oc,scl->sol", residue_filters[layer_index, 0], earlier, precision=lax.Precision.HIGHEST)
        mixing = mixing + jnp.einsum("oc,scl->sol", residue_filters[layer_index, 1], hidden, precision=lax.Precision.HIGHEST)
        mixing = mixing + jnp.einsum("oc,scl->sol", residue_filters[layer_index, 2], latter, precision=lax.Precision.HIGHEST)
        hidden = hidden + jax.nn.elu(mixing)
    weights = gap_mask.astype(jnp.float32)
    feature = (hidden * weights[:, None, :]).astype(jnp.bfloat16)
    return feature, weights


def pair_conv(padded, kernel, spread, offset, rows_out, cols_out):
    summed = jnp.zeros((rows_out * cols_out, kernel.shape[3]), jnp.float32)
    anchor = jnp.zeros((), jnp.int32)
    for row_tap in range(3):
        for col_tap in range(3):
            start_row = (offset + (row_tap - 1) * spread).astype(jnp.int32)
            start_col = (offset + (col_tap - 1) * spread).astype(jnp.int32)
            window = lax.dynamic_slice(padded, (start_row, start_col, anchor), (rows_out, cols_out, padded.shape[2]))
            summed = summed + jnp.dot(window.reshape(rows_out * cols_out, padded.shape[2]), kernel[row_tap, col_tap], preferred_element_type=jnp.float32)
    return summed.reshape(rows_out, cols_out, kernel.shape[3])


def reference(tokens, gap_mask, dilations, embedding, residue_filters, projection, pair_filters):
    feature, weights = residue_stack(tokens, gap_mask, dilations, embedding, residue_filters)
    length = tokens.shape[1]
    channels = embedding.shape[1]
    widened = feature.astype(jnp.float32)
    counts = jnp.dot(weights.T, weights, precision=lax.Precision.HIGHEST)

    def one_block(start):
        rows_part = lax.dynamic_slice_in_dim(widened, start, 4, 2)
        outer_sum = jnp.einsum("sai,sbj->ijab", rows_part, widened, precision=lax.Precision.HIGHEST)
        shared = lax.dynamic_slice_in_dim(counts, start, 4, 0)
        scaled = (outer_sum / (shared[:, :, None, None] + 1.0)).astype(jnp.bfloat16)
        projected = jnp.dot(scaled.reshape(4 * length, channels * channels), projection, preferred_element_type=jnp.float32)
        return projected.astype(jnp.bfloat16)

    starts = jnp.arange(length // 4, dtype=jnp.int32) * 4
    pair_input = lax.map(one_block, starts).reshape(length, length, projection.shape[1])
    padded = jnp.pad(pair_input, ((DMAX, DMAX), (DMAX, DMAX), (0, 0)))
    hidden_map = jax.nn.elu(pair_conv(padded, pair_filters[0], dilations[NL1], DMAX, length, length)).astype(jnp.bfloat16)
    padded_hidden = jnp.pad(hidden_map, ((DMAX, DMAX), (DMAX, DMAX), (0, 0)))
    second = pair_conv(padded_hidden, pair_filters[1], dilations[NL1 + 1], DMAX, length, length)
    return (pair_input.astype(jnp.float32) + second).astype(jnp.bfloat16)
```

```python
import functools

import jax
import jax.numpy as jnp
from jax import lax
from jax.experimental import pallas as pl
from jax.experimental.pallas import tpu as pltpu
from jax.sharding import PartitionSpec as P

NL1 = 2
DMAX = 4
HALO = 2 * DMAX
VMEM_LIMIT = 62 << 20


def elu(x):
    return jnp.maximum(x, jnp.exp(jnp.minimum(x, 0.0)) - 1.0)


def contract_last(left, right):
    return lax.dot_general(
        left, right, (((1,), (1,)), ((), ())), preferred_element_type=jnp.float32
    )


def exchange(block, axis, bit):
    count = lax.axis_size(axis)
    return lax.ppermute(block, axis, [(i, i ^ bit) for i in range(count)])


def gather_sequences(tokens, gap_mask):
    own = jnp.stack([tokens, gap_mask]).astype(jnp.bfloat16)[None]
    count = lax.axis_size("row")
    pair = jnp.concatenate([own, exchange(own, "row", 1)]) if count > 1 else own
    parts = [pair] + [exchange(pair, "row", bit) for bit in range(2, count, 2)]
    half = jnp.concatenate(parts)
    return jnp.concatenate([half, exchange(half, "col", 1)])


def feature_tables(embedding, filters):
    letters, channels = embedding.shape
    kinds = -(-letters // 32) * 32
    padded = jnp.pad(embedding, ((0, kinds - letters), (0, 0)))
    mixed = jnp.einsum("koc,tc->okt", filters[0], padded, precision=lax.Precision.HIGHEST)
    plain = jnp.zeros_like(mixed).at[:, 1, :].set(padded.T)
    table = jnp.concatenate([mixed, plain], axis=0).reshape(2 * channels, 3 * kinds)
    high = table.astype(jnp.bfloat16)
    low = (table - high.astype(jnp.float32)).astype(jnp.bfloat16)
    second = filters[1].transpose(1, 0, 2).reshape(channels, 3 * channels).astype(jnp.bfloat16)
    return jnp.concatenate([high, low], axis=1), second


def feature_kernel(
    scalars, seq_ref, table_ref, second_ref, row_ref, col_ref, row_mark_ref, col_mark_ref,
    token_s, mark_s, onehot_s, hidden_s, narrow_s, turn_s, *, unroll, pitch,
):
    first_spread, second_spread, row_first, col_first = scalars[0], scalars[1], scalars[2], scalars[3]
    blocks, _, each, length = seq_ref.shape
    width = blocks * each
    channels = second_ref.shape[0]
    kinds = onehot_s.shape[1]
    rows, cols = row_ref.shape[0], col_ref.shape[1]
    lanes = 128
    tokens = seq_ref[:, 0].reshape(width, length).astype(jnp.float32)
    marks = seq_ref[:, 1].reshape(width, length).astype(jnp.float32)
    token_s[HALO : HALO + length, :] = tokens.T
    mark_s[...] = marks.T
    edge = jnp.full((HALO, width), -1.0, jnp.float32)
    token_s[0:HALO, :] = edge
    token_s[HALO + length : 2 * HALO + length, :] = edge
    row_mark_ref[...] = mark_s[pl.ds(pl.multiple_of(row_first, 8), rows), :].astype(row_mark_ref.dtype)
    col_mark_ref[...] = mark_s[pl.ds(pl.multiple_of(col_first, 8), cols), :].astype(col_mark_ref.dtype)
    letters = lax.broadcasted_iota(jnp.int32, (kinds, width), 0).astype(jnp.float32)
    table = table_ref[...]
    second = second_ref[...]

    def run(first, count, emit):
        def hot(step, carry):
            block = token_s[pl.ds(pl.multiple_of(first + step * 8, 8), 8), :]
            for k in range(8):
                onehot_s[step * 8 + k] = jnp.where(block[k : k + 1, :] == letters, 1.0, 0.0).astype(onehot_s.dtype)
            return carry

        lax.fori_loop(0, (count + 2 * HALO) // 8, hot, 0)

        def one(step, carry):
            for k in range(unroll):
                at = DMAX + step * unroll + k
                taps = jnp.concatenate(
                    [onehot_s[at - first_spread], onehot_s[at], onehot_s[at + first_spread]], axis=0
                )
                mixing = jnp.dot(table, jnp.concatenate([taps, taps], axis=0), preferred_element_type=jnp.float32)
                hidden = mixing[channels:] + elu(mixing[:channels])
                hidden_s[at] = hidden
                narrow_s[at] = hidden.astype(narrow_s.dtype)
            return carry

        lax.fori_loop(0, (count + 2 * DMAX) // unroll, one, 0)
        nothing = jnp.zeros((channels, width), narrow_s.dtype)
        for k in range(DMAX):
            for at in (DMAX + k, count + HALO + k):
                place = first - HALO + at

                @pl.when((place < 0) | (place >= length))
                def _():
                    narrow_s[at] = nothing

        def two(step, carry):
            for k in range(unroll):
                index = step * unroll + k
                at = HALO + index
                taps = jnp.concatenate(
                    [narrow_s[at - second_spread], narrow_s[at], narrow_s[at + second_spread]], axis=0
                )
                mixing = jnp.dot(second, taps, preferred_element_type=jnp.float32)
                emit(index, (hidden_s[at] + elu(mixing)) * mark_s[pl.ds(first + index, 1), :])
            return carry

        lax.fori_loop(0, count // unroll, two, 0)

    def emit_row(index, value):
        row_ref[index] = value.astype(row_ref.dtype)

    def emit_col(index, value):
        for part in range(width // lanes):
            turn_s[pl.ds(part * channels * pitch + index, channels, stride=pitch), :] = value[
                :, part * lanes : (part + 1) * lanes
            ]

    run(row_first, rows, emit_row)
    run(col_first, cols, emit_col)

    def flush(channel, carry):
        for part in range(width // lanes):
            start = pl.multiple_of((part * channels + channel) * pitch, 8)
            col_ref[channel, :, part * lanes : (part + 1) * lanes] = turn_s[pl.ds(start, cols), :].astype(col_ref.dtype)
        return carry

    lax.fori_loop(0, channels, flush, 0)


def features(scalars, sequences, table, second, rows, cols, width=256, unroll=8):
    blocks, _, each, length = sequences.shape
    total = blocks * each
    channels = second.shape[0]
    kinds = table.shape[1] // 6
    span = max(rows, cols) + 2 * HALO
    pitch = cols + 8
    bf16, f32 = jnp.bfloat16, jnp.float32
    return pl.pallas_call(
        functools.partial(feature_kernel, unroll=unroll, pitch=pitch),
        grid_spec=pltpu.PrefetchScalarGridSpec(
            num_scalar_prefetch=1,
            grid=(total // width,),
            in_specs=[
                pl.BlockSpec((width // each, 2, each, length), lambda g, s: (g, 0, 0, 0)),
                pl.BlockSpec(table.shape, lambda g, s: (0, 0)),
                pl.BlockSpec(second.shape, lambda g, s: (0, 0)),
            ],
            out_specs=[
                pl.BlockSpec((rows, channels, width), lambda g, s: (0, 0, g)),
                pl.BlockSpec((channels, cols, width), lambda g, s: (0, 0, g)),
                pl.BlockSpec((rows, width), lambda g, s: (0, g)),
                pl.BlockSpec((cols, width), lambda g, s: (0, g)),
            ],
            scratch_shapes=[
                pltpu.VMEM((length + 2 * HALO, width), f32),
                pltpu.VMEM((length, width), f32),
                pltpu.VMEM((span, kinds, width), bf16),
                pltpu.VMEM((span, channels, width), f32),
                pltpu.VMEM((span, channels, width), bf16),
                pltpu.VMEM((width // 128 * channels * pitch, 128), f32),
            ],
        ),
        out_shape=[
            jax.ShapeDtypeStruct((rows, channels, total), bf16),
            jax.ShapeDtypeStruct((channels, cols, total), bf16),
            jax.ShapeDtypeStruct((rows, total), bf16),
            jax.ShapeDtypeStruct((cols, total), bf16),
        ],
        compiler_params=pltpu.CompilerParams(vmem_limit_bytes=VMEM_LIMIT),
    )(scalars, sequences, table, second)


def outer_kernel(row_ref, col_ref, projection_ref, row_mark_ref, col_mark_ref, pair_ref, sum_s, *, chunk):
    step = pl.program_id(0)
    rows, channels, total = row_ref.shape
    group, cols, _ = col_ref.shape

    @pl.when(step == 0)
    def _():
        sum_s[...] = jnp.zeros_like(sum_s)

    right = col_ref[...].reshape(group * cols, total)
    projection = projection_ref[...]
    for base in range(0, rows, chunk):
        left = row_ref[base : base + chunk].reshape(chunk * channels, total)
        outer = contract_last(left, right).astype(jnp.bfloat16)
        for pair in range(0, chunk, 2):
            halves = [
                jnp.concatenate(
                    [outer[i * channels : (i + 1) * channels, b * cols : (b + 1) * cols] for b in range(group)], axis=0
                )
                for i in (pair, pair + 1)
            ]
            sum_s[(base + pair) // 2] += jnp.dot(
                projection, jnp.concatenate(halves, axis=1), preferred_element_type=jnp.float32
            )

    @pl.when(step == pl.num_programs(0) - 1)
    def _():
        counts = contract_last(row_mark_ref[...], col_mark_ref[...])
        share = 1.0 / (counts + 1.0)
        for i in range(rows):
            value = sum_s[i // 2][:, (i % 2) * cols : (i % 2 + 1) * cols] * share[i : i + 1, :]
            pair_ref[i] = value.T.astype(pair_ref.dtype)


def outer_products(row_feat, col_feat, projection, row_marks, col_marks, group=8, chunk=16):
    rows, channels, total = row_feat.shape
    cols = col_feat.shape[1]
    out = projection.shape[0]
    return pl.pallas_call(
        functools.partial(outer_kernel, chunk=min(chunk, rows)),
        grid=(channels // group,),
        in_specs=[
            pl.BlockSpec((rows, channels, total), lambda g: (0, 0, 0)),
            pl.BlockSpec((group, cols, total), lambda g: (g, 0, 0)),
            pl.BlockSpec((out, group * channels), lambda g: (0, g)),
            pl.BlockSpec((rows, total), lambda g: (0, 0)),
            pl.BlockSpec((cols, total), lambda g: (0, 0)),
        ],
        out_specs=pl.BlockSpec((rows, cols, out), lambda g: (0, 0, 0)),
        out_shape=jax.ShapeDtypeStruct((rows, cols, out), jnp.bfloat16),
        scratch_shapes=[pltpu.VMEM((rows // 2, out, 2 * cols), jnp.float32)],
        compiler_params=pltpu.CompilerParams(vmem_limit_bytes=VMEM_LIMIT),
        cost_estimate=pl.CostEstimate(
            flops=2 * rows * cols * channels * channels * (total + out),
            bytes_accessed=2 * channels * total * (rows + cols),
            transcendentals=0,
        ),
    )(row_feat, col_feat, projection, row_marks, col_marks)


def conv_kernel(
    scalars, above_ref, own_ref, below_ref, left_ref, right_ref, filter_ref, out_ref, wide_s, tap_s, hidden_s, *, length
):
    first_spread, second_spread, row_first, col_first = scalars[0], scalars[1], scalars[2], scalars[3]
    rows, cols, channels = out_ref.shape
    tall, broad = rows + 2 * DMAX, cols + 2 * DMAX
    f32, bf16 = jnp.float32, jnp.bfloat16
    wide_s[0:HALO, HALO : HALO + cols, :] = above_ref[...].astype(f32)
    wide_s[HALO : HALO + rows, HALO : HALO + cols, :] = own_ref[...].astype(f32)
    wide_s[HALO + rows : 2 * HALO + rows, HALO : HALO + cols, :] = below_ref[...].astype(f32)
    wide_s[:, 0:HALO, :] = left_ref[...].astype(f32)
    wide_s[:, HALO + cols : 2 * HALO + cols, :] = right_ref[...].astype(f32)

    def spread_taps(source, count, start, spread, width):
        def body(i, carry):
            for tap in range(3):
                piece = source[i, pl.ds(start + (tap - 1) * spread, width), :]
                tap_s[i, 0:width, tap * channels : (tap + 1) * channels] = piece.astype(bf16)
            return carry

        lax.fori_loop(0, count, body, 0)

    spread_taps(wide_s, rows + 2 * HALO, DMAX, first_spread, broad)
    first = filter_ref[0]
    places = col_first - DMAX + lax.broadcasted_iota(jnp.int32, (broad, channels), 0)
    col_inside = ((places >= 0) & (places < length)).astype(f32)

    def one(i, carry):
        at = i + DMAX
        taps = jnp.concatenate(
            [tap_s[at - first_spread, 0:broad], tap_s[at, 0:broad], tap_s[at + first_spread, 0:broad]], axis=1
        )
        mixing = elu(jnp.dot(taps, first, preferred_element_type=f32)).astype(bf16).astype(f32)
        place = row_first - DMAX + i
        hidden_s[i] = mixing * col_inside * jnp.where((place >= 0) & (place < length), 1.0, 0.0)
        return carry

    lax.fori_loop(0, tall, one, 0, unroll=4)
    spread_taps(hidden_s, tall, DMAX, second_spread, cols)
    second = filter_ref[1]

    def two(i, carry):
        at = i + DMAX
        taps = jnp.concatenate(
            [tap_s[at - second_spread, 0:cols], tap_s[at, 0:cols], tap_s[at + second_spread, 0:cols]], axis=1
        )
        mixing = jnp.dot(taps, second, preferred_element_type=f32)
        out_ref[i] = (own_ref[i].astype(f32) + mixing).astype(out_ref.dtype)
        return carry

    lax.fori_loop(0, rows, two, 0, unroll=4)


def pair_convolutions(scalars, above, own, below, left, right, filters, length):
    rows, cols, channels = own.shape
    tall, broad = rows + 2 * HALO, cols + 2 * HALO
    whole = lambda array: pl.BlockSpec(array.shape, functools.partial(lambda rank, g, s: (0,) * rank, array.ndim))
    return pl.pallas_call(
        functools.partial(conv_kernel, length=length),
        grid_spec=pltpu.PrefetchScalarGridSpec(
            num_scalar_prefetch=1,
            grid=(1,),
            in_specs=[whole(x) for x in (above, own, below, left, right, filters)],
            out_specs=whole(own),
            scratch_shapes=[
                pltpu.VMEM((tall, broad, channels), jnp.float32),
                pltpu.VMEM((tall, broad - 2 * DMAX, 3 * channels), jnp.bfloat16),
                pltpu.VMEM((tall - 2 * DMAX, broad - 2 * DMAX, channels), jnp.float32),
            ],
        ),
        out_shape=jax.ShapeDtypeStruct(own.shape, own.dtype),
        compiler_params=pltpu.CompilerParams(vmem_limit_bytes=VMEM_LIMIT),
    )(scalars, above, own, below, left, right, filters)


def col_margins(tall):
    count = lax.axis_size("col")
    head, tail = tall[:, :HALO], tall[:, tall.shape[1] - HALO :]
    if count == 2:
        here = lax.axis_index("col")
        got = lax.ppermute(jnp.where(here == 0, tail, head), "col", [(0, 1), (1, 0)])
        nothing = jnp.zeros_like(got)
        return jnp.where(here == 0, nothing, got), jnp.where(here == 0, got, nothing)
    steps = range(count - 1)
    return (
        lax.ppermute(tail, "col", [(i, i + 1) for i in steps]),
        lax.ppermute(head, "col", [(i + 1, i) for i in steps]),
    )


def row_margins(head, tail):
    steps = range(lax.axis_size("row") - 1)
    return (
        lax.ppermute(tail, "row", [(i, i + 1) for i in steps]),
        lax.ppermute(head, "row", [(i + 1, i) for i in steps]),
    )


def per_device(tokens, gap_mask, dilations, embedding, residue_filters, projection, pair_filters):
    length = tokens.shape[1]
    channels = embedding.shape[1]
    out = projection.shape[1]
    rows = length // lax.axis_size("row")
    cols = length // lax.axis_size("col")
    starts = jnp.stack([lax.axis_index("row") * rows, lax.axis_index("col") * cols]).astype(jnp.int32)
    sequences = gather_sequences(tokens, gap_mask)
    table, second = feature_tables(embedding, residue_filters)
    row_feat, col_feat, row_marks, col_marks = features(
        jnp.concatenate([dilations[:NL1], starts]), sequences, table, second, rows, cols
    )
    turned = projection.reshape(channels, channels, out).transpose(2, 1, 0).reshape(out, channels * channels)
    if rows > 2 * HALO:
        ends = jnp.concatenate([row_feat[:HALO], row_feat[rows - HALO :]])
        end_marks = jnp.concatenate([row_marks[:HALO], row_marks[rows - HALO :]])
        outside = outer_products(ends, col_feat, turned, end_marks, col_marks)
        above, below = row_margins(outside[:HALO], outside[HALO:])
        inside = outer_products(
            row_feat[HALO : rows - HALO], col_feat, turned, row_marks[HALO : rows - HALO], col_marks
        )
        own = jnp.concatenate([outside[:HALO], inside, outside[HALO:]])
    else:
        own = outer_products(row_feat, col_feat, turned, row_marks, col_marks)
        above, below = row_margins(own[:HALO], own[rows - HALO :])
    left, right = col_margins(jnp.concatenate([above, own, below]))
    return pair_convolutions(
        jnp.concatenate([dilations[NL1:], starts]),
        above, own, below, left, right,
        pair_filters.reshape(2, 9 * pair_filters.shape[3], pair_filters.shape[4]),
        length,
    )


def solution(mesh):
    in_specs = (
        P(("grp", "row", "col"), None),
        P(("grp", "row", "col"), None),
        P(),
        P(),
        P(),
        P(),
        P(),
    )
    out_specs = P(("grp", "row"), "col", None)
    return jax.shard_map(per_device, mesh=mesh, in_specs=in_specs, out_specs=out_specs, check_vma=False)
```

```python
import functools

import jax
import jax.numpy as jnp
from jax import lax
from jax.experimental import pallas as pl
from jax.experimental.pallas import tpu as pltpu
from jax.sharding import PartitionSpec as P


NL1 = 2
DMAX = 4
HALO = 2 * DMAX
BLOCK = 16
VMEM_LIMIT = 62 << 20


def elu(x):
    return jnp.maximum(x, jnp.exp(jnp.minimum(x, 0.0)) - 1.0)


def contract_last(left, right):
    return lax.dot_general(
        left, right, (((1,), (1,)), ((), ())), preferred_element_type=jnp.float32
    )


def exchange(block, axis, bit):
    count = lax.axis_size(axis)
    return lax.ppermute(block, axis, [(i, i ^ bit) for i in range(count)])


def first_sequences(tokens, gap_mask):
    half = jnp.stack([tokens, gap_mask]).astype(jnp.bfloat16)[None]
    bit = lax.axis_size("row") // 4
    while bit >= 1:
        half = jnp.concatenate([half, exchange(half, "row", bit)])
        bit //= 2
    return half


def feature_tables(embedding, filters):
    letters, channels = embedding.shape
    kinds = -(-letters // 32) * 32
    padded = jnp.pad(embedding, ((0, kinds - letters), (0, 0)))
    mixed = jnp.einsum("koc,tc->okt", filters[0], padded, precision=lax.Precision.HIGHEST)
    plain = jnp.zeros_like(mixed).at[:, 1, :].set(padded.T)
    table = jnp.concatenate([mixed, plain], axis=0).reshape(2 * channels, 3 * kinds)
    high = table.astype(jnp.bfloat16)
    low = (table - high.astype(jnp.float32)).astype(jnp.bfloat16)
    second = filters[1].transpose(1, 0, 2).reshape(channels, 3 * channels).astype(jnp.bfloat16)
    return jnp.concatenate([high, low], axis=1), second


def feature_kernel(
    scalars, here_ref, there_ref, table_ref, second_ref, row_ref, col_ref, row_mark_ref, col_mark_ref,
    token_s, mark_s, onehot_s, hidden_s, narrow_s, turn_s, stage_s, sems, *, pitch,
):
    first_spread, second_spread, row_first, col_first = scalars[0], scalars[1], scalars[2], scalars[3]
    blocks, _, each, length = here_ref.shape
    part = blocks * each
    width = 2 * part
    channels = second_ref.shape[0]
    kinds = onehot_s.shape[1]
    rows, cols = row_ref.shape[0], col_ref.shape[1]
    lanes = 128
    for side, ref in enumerate((here_ref, there_ref)):
        at = slice(side * part, (side + 1) * part)
        token_s[HALO : HALO + length, at] = ref[:, 0].reshape(part, length).astype(jnp.float32).T
        mark_s[:, at] = ref[:, 1].reshape(part, length).astype(jnp.float32).T
    edge = jnp.full((HALO, width), -1.0, jnp.float32)
    token_s[0:HALO, :] = edge
    token_s[HALO + length : 2 * HALO + length, :] = edge
    row_mark_ref[...] = mark_s[pl.ds(pl.multiple_of(row_first, 8), rows), :].astype(row_mark_ref.dtype)
    col_mark_ref[...] = mark_s[pl.ds(pl.multiple_of(col_first, 8), cols), :].astype(col_mark_ref.dtype)
    letters = lax.broadcasted_iota(jnp.int32, (kinds, width), 0).astype(jnp.float32)
    table = table_ref[...]
    second = second_ref[...]

    def layer_one(start, count):
        for k in range(count):
            at = start + k
            taps = jnp.concatenate([onehot_s[at - first_spread], onehot_s[at], onehot_s[at + first_spread]], axis=0)
            mixing = jnp.dot(table, jnp.concatenate([taps, taps], axis=0), preferred_element_type=jnp.float32)
            hidden = mixing[channels:] + elu(mixing[:channels])
            hidden_s[at] = hidden
            narrow_s[at] = hidden.astype(narrow_s.dtype)

    def run(first, count, emit, finish):
        def hot(step, carry):
            block = token_s[pl.ds(pl.multiple_of(first + step * 8, 8), 8), :]
            for k in range(8):
                onehot_s[step * 8 + k] = jnp.where(block[k : k + 1, :] == letters, 1.0, 0.0).astype(onehot_s.dtype)
            return carry

        lax.fori_loop(0, (count + 2 * HALO) // 8, hot, 0)

        def layer_two(step):
            marks = mark_s[pl.ds(pl.multiple_of(first + step * BLOCK, 8), BLOCK), :]
            for k in range(BLOCK):
                at = HALO + step * BLOCK + k
                taps = jnp.concatenate(
                    [narrow_s[at - second_spread], narrow_s[at], narrow_s[at + second_spread]], axis=0
                )
                mixing = jnp.dot(second, taps, preferred_element_type=jnp.float32)
                emit(step, k, (hidden_s[at] + elu(mixing)) * marks[k : k + 1, :])
            finish(step)

        def clear(starts):
            for start in starts:
                for k in range(DMAX):
                    place = first - HALO + start + k

                    @pl.when((place < 0) | (place >= length))
                    def _():
                        narrow_s[start + k] = jnp.zeros((channels, width), narrow_s.dtype)

        ahead = BLOCK + 2 * DMAX
        layer_one(DMAX, ahead)
        clear((DMAX,))

        def trip(step, carry):
            layer_two(step)
            layer_one(DMAX + ahead + step * BLOCK, BLOCK)
            return carry

        lax.fori_loop(0, count // BLOCK - 1, trip, 0)
        clear((count + HALO,))
        layer_two(count // BLOCK - 1)

    def emit_row(step, k, value):
        row_ref[step * BLOCK + k] = value.astype(row_ref.dtype)

    def emit_col(step, k, value):
        for piece in range(width // lanes):
            turn_s[pl.ds(piece * channels * pitch + k, channels, stride=pitch), :] = value[
                :, piece * lanes : (piece + 1) * lanes
            ]

    def leave(step):
        slot = lax.rem(step, 2)
        start = pl.multiple_of(step * BLOCK, BLOCK)
        return pltpu.make_async_copy(stage_s.at[slot], col_ref.at[:, pl.ds(start, BLOCK), :], sems.at[slot])

    def finish_col(step):
        @pl.when(step >= 2)
        def _():
            leave(step - 2).wait()

        slot = lax.rem(step, 2)
        for channel in range(channels):
            for piece in range(width // lanes):
                start = (piece * channels + channel) * pitch
                stage_s[slot, channel, :, piece * lanes : (piece + 1) * lanes] = turn_s[
                    start : start + BLOCK, :
                ].astype(stage_s.dtype)
        leave(step).start()

    run(row_first, rows, emit_row, lambda step: None)
    run(col_first, cols, emit_col, finish_col)
    steps = cols // BLOCK
    for step in range(max(steps - 2, 0), steps):
        leave(step).wait()


def features(scalars, here, there, table, second, rows, cols):
    blocks, _, each, length = here.shape
    width = 2 * blocks * each
    channels = second.shape[0]
    kinds = table.shape[1] // 6
    span = max(rows, cols) + 2 * HALO
    pitch = BLOCK + 8
    bf16, f32 = jnp.bfloat16, jnp.float32
    full = lambda shape: pl.BlockSpec(shape, functools.partial(lambda rank, g, s: (0,) * rank, len(shape)))
    return pl.pallas_call(
        functools.partial(feature_kernel, pitch=pitch),
        grid_spec=pltpu.PrefetchScalarGridSpec(
            num_scalar_prefetch=1,
            grid=(1,),
            in_specs=[full(x.shape) for x in (here, there, table, second)],
            out_specs=[
                full((rows, channels, width)),
                pl.BlockSpec(memory_space=pl.ANY),
                full((rows, width)),
                full((cols, width)),
            ],
            scratch_shapes=[
                pltpu.VMEM((length + 2 * HALO, width), f32),
                pltpu.VMEM((length, width), f32),
                pltpu.VMEM((span, kinds, width), bf16),
                pltpu.VMEM((span, channels, width), f32),
                pltpu.VMEM((span, channels, width), bf16),
                pltpu.VMEM((width // 128 * channels * pitch, 128), f32),
                pltpu.VMEM((2, channels, BLOCK, width), bf16),
                pltpu.SemaphoreType.DMA((2,)),
            ],
        ),
        out_shape=[
            jax.ShapeDtypeStruct((rows, channels, width), bf16),
            jax.ShapeDtypeStruct((channels, cols, width), bf16),
            jax.ShapeDtypeStruct((rows, width), bf16),
            jax.ShapeDtypeStruct((cols, width), bf16),
        ],
        compiler_params=pltpu.CompilerParams(vmem_limit_bytes=VMEM_LIMIT),
        cost_estimate=pl.CostEstimate(
            flops=40 * channels * channels * width * (rows + cols),
            bytes_accessed=2 * channels * width * (rows + cols),
            transcendentals=2 * channels * width * (rows + cols),
        ),
    )(scalars, here, there, table, second)


def outer_kernel(scalars, *refs, picks, halves, swap):
    count = len(picks)
    row_refs = refs[: halves * count]
    col_refs = refs[halves * count : halves * (count + 1)]
    projection_ref = refs[halves * (count + 1)]
    marks = refs[halves * (count + 1) + 1 : -(count + 2)]
    pair_refs = refs[-(count + 2) : -2]
    edge_ref, sum_s = refs[-2:]
    step = pl.program_id(0)
    group, cols, _ = col_refs[0].shape
    channels = row_refs[0].shape[1]
    rows = count * HALO

    @pl.when(step == 0)
    def _():
        sum_s[...] = jnp.zeros_like(sum_s)

    right = jnp.concatenate([ref[...].reshape(group * cols, ref.shape[2]) for ref in col_refs], axis=1)
    left = jnp.concatenate(
        [
            jnp.concatenate([row_refs[p * halves + h][...].reshape(HALO * channels, -1) for h in range(halves)], axis=1)
            for p in range(count)
        ],
        axis=0,
    )
    projection = projection_ref[...]
    outer = contract_last(left, right).astype(jnp.bfloat16)
    for pair in range(0, rows, 2):
        sides = [
            jnp.concatenate(
                [outer[i * channels : (i + 1) * channels, b * cols : (b + 1) * cols] for b in range(group)], axis=0
            )
            for i in (pair, pair + 1)
        ]
        sum_s[pair // 2] += jnp.dot(
            projection, jnp.concatenate(sides, axis=1), preferred_element_type=jnp.float32
        )

    @pl.when(step == pl.num_programs(0) - 1)
    def _():
        row_marks, col_marks = marks[:halves], marks[halves:]
        counts = sum(contract_last(r[...], c[...]) for r, c in zip(row_marks, col_marks))
        share = 1.0 / (counts + 1.0)
        for p, pick in enumerate(picks):
            for k in range(HALO):
                i = p * HALO + k
                place = pick * HALO + k
                value = sum_s[i // 2][:, (i % 2) * cols : (i % 2 + 1) * cols] * share[place : place + 1, :]
                value = value.T
                pair_refs[p][k] = value.astype(edge_ref.dtype)
                if swap:
                    edge_ref[i] = jnp.where(scalars[0] == 0, value[cols - HALO :], value[:HALO]).astype(edge_ref.dtype)
        if not swap:
            edge_ref[...] = jnp.zeros_like(edge_ref)


def outer_products(scalars, row_feats, col_feats, projection, row_marks, col_marks, picks, swap, group=8):
    _, channels, _ = row_feats[0].shape
    cols = col_feats[0].shape[1]
    out = projection.shape[0]
    total = sum(x.shape[2] for x in row_feats)
    tall = len(picks) * HALO
    full = lambda shape: pl.BlockSpec(shape, functools.partial(lambda rank, g, s: (0,) * rank, len(shape)))
    picked = lambda pick, width: pl.BlockSpec((HALO, channels, width), lambda g, s: (pick, 0, 0))
    results = pl.pallas_call(
        functools.partial(outer_kernel, picks=picks, halves=len(row_feats), swap=swap),
        grid_spec=pltpu.PrefetchScalarGridSpec(
            num_scalar_prefetch=1,
            grid=(channels // group,),
            in_specs=[picked(pick, x.shape[2]) for pick in picks for x in row_feats]
            + [pl.BlockSpec((group, cols, x.shape[2]), lambda g, s: (g, 0, 0)) for x in col_feats]
            + [pl.BlockSpec((out, group * channels), lambda g, s: (0, g))]
            + [full(x.shape) for x in (*row_marks, *col_marks)],
            out_specs=[full((HALO, cols, out)) for _ in picks] + [full((tall, HALO, out))],
            scratch_shapes=[pltpu.VMEM((tall // 2, out, 2 * cols), jnp.float32)],
        ),
        out_shape=[jax.ShapeDtypeStruct((HALO, cols, out), jnp.bfloat16) for _ in picks]
        + [jax.ShapeDtypeStruct((tall, HALO, out), jnp.bfloat16)],
        compiler_params=pltpu.CompilerParams(vmem_limit_bytes=VMEM_LIMIT),
        cost_estimate=pl.CostEstimate(
            flops=2 * tall * cols * channels * channels * (total + out),
            bytes_accessed=2 * channels * total * (tall + cols),
            transcendentals=0,
        ),
    )(
        scalars,
        *[x for _ in picks for x in row_feats],
        *col_feats,
        projection,
        *row_marks,
        *col_marks,
    )
    return list(results[:-1]), results[-1]


def conv_kernel(scalars, *refs, length, swap):
    first_spread, second_spread, row_first, col_first = scalars[0], scalars[1], scalars[2], scalars[3]
    row_refs = refs[:-8]
    left_ref, right_ref, edge_ref, filter_ref, out_ref, wide_s, tap_s, hidden_s = refs[-8:]
    rows, cols, channels = out_ref.shape
    tall, broad = rows + 2 * DMAX, cols + 2 * DMAX
    f32, bf16 = jnp.float32, jnp.bfloat16
    for block, ref in enumerate(row_refs):
        wide_s[block * HALO : (block + 1) * HALO, HALO : HALO + cols, :] = ref[...].astype(f32)
    if swap:
        edges = edge_ref[...].astype(f32)
        wide_s[:, 0:HALO, :] = jnp.where(col_first == 0, jnp.zeros_like(edges), edges)
        wide_s[:, HALO + cols : 2 * HALO + cols, :] = jnp.where(col_first == 0, edges, jnp.zeros_like(edges))
    else:
        wide_s[:, 0:HALO, :] = left_ref[...].astype(f32)
        wide_s[:, HALO + cols : 2 * HALO + cols, :] = right_ref[...].astype(f32)

    def spread_taps(source, count, start, spread, width):
        def body(i, carry):
            for tap in range(3):
                piece = source[i, pl.ds(start + (tap - 1) * spread, width), :]
                tap_s[i, 0:width, tap * channels : (tap + 1) * channels] = piece.astype(bf16)
            return carry

        lax.fori_loop(0, count, body, 0)

    spread_taps(wide_s, rows + 2 * HALO, DMAX, first_spread, broad)
    first = filter_ref[0]
    places = col_first - DMAX + lax.broadcasted_iota(jnp.int32, (broad, channels), 0)
    col_inside = ((places >= 0) & (places < length)).astype(f32)

    def one(i, carry):
        at = i + DMAX
        taps = jnp.concatenate(
            [tap_s[at - first_spread, 0:broad], tap_s[at, 0:broad], tap_s[at + first_spread, 0:broad]], axis=1
        )
        mixing = elu(jnp.dot(taps, first, preferred_element_type=f32)).astype(bf16).astype(f32)
        place = row_first - DMAX + i
        hidden_s[i] = mixing * col_inside * jnp.where((place >= 0) & (place < length), 1.0, 0.0)
        return carry

    lax.fori_loop(0, tall, one, 0, unroll=4)
    spread_taps(hidden_s, tall, DMAX, second_spread, cols)
    second = filter_ref[1]

    def two(i, carry):
        at = i + DMAX
        taps = jnp.concatenate(
            [tap_s[at - second_spread, 0:cols], tap_s[at, 0:cols], tap_s[at + second_spread, 0:cols]], axis=1
        )
        mixing = jnp.dot(taps, second, preferred_element_type=f32)
        own = wide_s[i + HALO, HALO : HALO + cols, :]
        out_ref[i] = (own + mixing).astype(out_ref.dtype)
        return carry

    lax.fori_loop(0, rows, two, 0, unroll=4)


def pair_convolutions(scalars, blocks, left, right, edges, filters, length, swap):
    cols, channels = blocks[0].shape[1:]
    rows = (len(blocks) - 2) * HALO
    tall, broad = rows + 2 * HALO, cols + 2 * HALO
    operands = (*blocks, left, right, edges, filters)
    full = lambda shape: pl.BlockSpec(shape, functools.partial(lambda rank, g, s: (0,) * rank, len(shape)))
    return pl.pallas_call(
        functools.partial(conv_kernel, length=length, swap=swap),
        grid_spec=pltpu.PrefetchScalarGridSpec(
            num_scalar_prefetch=1,
            grid=(1,),
            in_specs=[full(x.shape) for x in operands],
            out_specs=full((rows, cols, channels)),
            scratch_shapes=[
                pltpu.VMEM((tall, broad, channels), jnp.float32),
                pltpu.VMEM((tall, broad - 2 * DMAX, 3 * channels), jnp.bfloat16),
                pltpu.VMEM((tall - 2 * DMAX, broad - 2 * DMAX, channels), jnp.float32),
            ],
        ),
        out_shape=jax.ShapeDtypeStruct((rows, cols, channels), jnp.bfloat16),
        compiler_params=pltpu.CompilerParams(vmem_limit_bytes=VMEM_LIMIT),
    )(scalars, *operands)


def col_margins(tall):
    steps = range(lax.axis_size("col") - 1)
    head, tail = tall[:, :HALO], tall[:, tall.shape[1] - HALO :]
    return (
        lax.ppermute(tail, "col", [(i, i + 1) for i in steps]),
        lax.ppermute(head, "col", [(i + 1, i) for i in steps]),
    )


def per_device(tokens, gap_mask, dilations, embedding, residue_filters, projection, pair_filters):
    length = tokens.shape[1]
    channels = embedding.shape[1]
    out = projection.shape[1]
    row_count, col_count = lax.axis_size("row"), lax.axis_size("col")
    rows, cols = length // row_count, length // col_count
    col_index = lax.axis_index("col")
    starts = jnp.stack([lax.axis_index("row") * rows, col_index * cols]).astype(jnp.int32)
    col_scalar = col_index.astype(jnp.int32).reshape(1)
    swap = col_count == 2
    near = first_sequences(tokens, gap_mask)
    near_there = exchange(near, "col", 1)
    far = exchange(near, "row", row_count // 2)
    far_there = exchange(far, "col", 1)
    table, second = feature_tables(embedding, residue_filters)
    turned = projection.reshape(channels, channels, out).transpose(2, 1, 0).reshape(out, channels * channels)
    scalars = jnp.concatenate([dilations[:NL1], starts])
    near_parts = features(scalars, near, near_there, table, second, rows, cols)
    far_parts = features(scalars, far, far_there, table, second, rows, cols)
    row_feats, col_feats, row_marks, col_marks = zip(near_parts, far_parts)
    last = rows // HALO - 1
    run = functools.partial(outer_products, col_scalar, row_feats, col_feats, turned, row_marks, col_marks, swap=swap)
    ends, end_edges = run(picks=(0, last))
    steps = range(row_count - 1)
    above = lax.ppermute(ends[1], "row", [(i, i + 1) for i in steps])
    below = lax.ppermute(ends[0], "row", [(i + 1, i) for i in steps])
    if last > 1:
        middle, middle_edges = run(picks=tuple(range(1, last)))
    else:
        middle, middle_edges = [], end_edges[:0]
    blocks = [above, ends[0], *middle, ends[1], below]
    if swap:
        pick = lambda block: jnp.where(col_index == 0, block[:, cols - HALO :], block[:, :HALO])
        edges = jnp.concatenate([pick(above), end_edges[:HALO], middle_edges, end_edges[HALO:], pick(below)])
        edges = exchange(edges, "col", 1)
        left = right = edges[:1]
    else:
        left, right = col_margins(jnp.concatenate(blocks))
        edges = left[:1]
    return pair_convolutions(
        jnp.concatenate([dilations[NL1:], starts]),
        blocks, left, right, edges,
        pair_filters.reshape(2, 9 * pair_filters.shape[3], pair_filters.shape[4]),
        length,
        swap,
    )


def solution(mesh):
    in_specs = (
        P(("grp", "row", "col"), None),
        P(("grp", "row", "col"), None),
        P(),
        P(),
        P(),
        P(),
        P(),
    )
    out_specs = P(("grp", "row"), "col", None)
    return jax.shard_map(per_device, mesh=mesh, in_specs=in_specs, out_specs=out_specs, check_vma=False)
```

```python
import functools
import math

import jax
import jax.numpy as jnp
from jax import lax
from jax.experimental import pallas as pl
from jax.experimental.pallas import tpu as pltpu
from jax.sharding import PartitionSpec as P


NL1 = 2
DMAX = 4
HALO = 2 * DMAX
BLOCK = 16
LANES = 128
TILE = 256
LOG2E = 1.4426950408889634
SHIFT = math.log2(LOG2E)
VMEM_LIMIT = 62 << 20


def elu(x):
    return jnp.maximum(x, jnp.exp(jnp.minimum(x, 0.0)) - 1.0)


def contract_last(left, right):
    return lax.dot_general(
        left, right, (((1,), (1,)), ((), ())), preferred_element_type=jnp.float32
    )


def exchange(block, axis, bit):
    count = lax.axis_size(axis)
    return lax.ppermute(block, axis, [(i, i ^ bit) for i in range(count)])


def first_sequences(tokens, gap_mask):
    half = jnp.stack([tokens, gap_mask]).astype(jnp.bfloat16)[None]
    bit = lax.axis_size("row") // 4
    while bit >= 1:
        half = jnp.concatenate([half, exchange(half, "row", bit)])
        bit //= 2
    return half


def prepare_kernel(embedding_ref, filters_ref, projection_ref, table_ref, second_ref, turned_ref, letter_s, turn_s):
    letters, channels = embedding_ref.shape
    kinds = letter_s.shape[0]
    f32, bf16 = jnp.float32, jnp.bfloat16
    letter_s[...] = jnp.zeros_like(letter_s)
    letter_s[0:letters, :] = embedding_ref[...]
    letter = letter_s[...]
    for tap in range(3):
        mixed = LOG2E * lax.dot_general(
            filters_ref[0, tap], letter, (((1,), (1,)), ((), ())),
            precision=lax.Precision.HIGHEST, preferred_element_type=f32,
        )
        plain = jnp.zeros((channels, kinds), f32)
        if tap == 1:
            mixed = mixed + SHIFT
            plain = LOG2E * letter.T - SHIFT
        for first, value in ((0, mixed), (channels, plain)):
            high = value.astype(bf16)
            low = (value - high.astype(f32)).astype(bf16)
            for part, piece in enumerate((high, low)):
                start = (part * 3 + tap) * kinds
                table_ref[first : first + channels, start : start + kinds] = piece
        second_ref[:, tap * channels : (tap + 1) * channels] = filters_ref[1, tap].astype(bf16)
    pitch = turn_s.shape[0] // channels

    def widen(a, carry):
        start = pl.multiple_of(a * channels, channels)
        turn_s[pl.ds(pl.multiple_of(a * pitch, 8), channels), :] = projection_ref[pl.ds(start, channels), :].astype(f32)
        return carry

    lax.fori_loop(0, channels, widen, 0, unroll=4)

    def turn(step, carry):
        pair = jnp.concatenate([turn_s[pl.ds(2 * step + k, channels, stride=pitch), :] for k in range(2)], axis=0)
        start = pl.multiple_of(step * 2 * channels, 2 * channels)
        turned_ref[:, pl.ds(start, 2 * channels)] = pair.T.astype(bf16)
        return carry

    lax.fori_loop(0, channels // 2, turn, 0, unroll=2)


def prepare(embedding, filters, projection):
    letters, channels = embedding.shape
    kinds = -(-letters // 32) * 32
    out = projection.shape[1]
    bf16 = jnp.bfloat16
    return pl.pallas_call(
        prepare_kernel,
        out_shape=[
            jax.ShapeDtypeStruct((2 * channels, 6 * kinds), bf16),
            jax.ShapeDtypeStruct((channels, 3 * channels), bf16),
            jax.ShapeDtypeStruct((out, channels * channels), bf16),
        ],
        scratch_shapes=[
            pltpu.VMEM((kinds, channels), jnp.float32),
            pltpu.VMEM((channels * (channels + 8), out), jnp.float32),
        ],
        compiler_params=pltpu.CompilerParams(vmem_limit_bytes=16 << 20),
        cost_estimate=pl.CostEstimate(flops=10**6, bytes_accessed=4 << 20, transcendentals=0),
    )(embedding, filters, projection)


def feature_kernel(
    dilations, here_ref, there_ref, table_ref, second_ref, row_ref, col_ref, row_mark_ref, col_mark_ref,
    token_s, mark_s, onehot_s, hidden_s, narrow_s, turn_s, stage_s, sems, *, pitch,
):
    first_spread, second_spread = dilations[0], dilations[1]
    blocks, _, each, length = here_ref.shape
    part = blocks * each
    width = 2 * part
    channels = second_ref.shape[0]
    kinds = onehot_s.shape[1]
    rows, cols = row_ref.shape[0], col_ref.shape[1]
    row_first, col_first = lax.axis_index("row") * rows, lax.axis_index("col") * cols
    lanes = LANES
    for side, ref in enumerate((here_ref, there_ref)):
        at = slice(side * part, (side + 1) * part)
        token_s[HALO : HALO + length, at] = ref[:, 0].reshape(part, length).astype(jnp.float32).T
        mark_s[:, at] = ref[:, 1].reshape(part, length).astype(jnp.float32).T
    edge = jnp.full((HALO, width), -1.0, jnp.float32)
    token_s[0:HALO, :] = edge
    token_s[HALO + length : 2 * HALO + length, :] = edge
    row_mark_ref[...] = mark_s[pl.ds(pl.multiple_of(row_first, 8), rows), :].astype(row_mark_ref.dtype)
    col_mark_ref[...] = mark_s[pl.ds(pl.multiple_of(col_first, 8), cols), :].astype(col_mark_ref.dtype)
    letters = lax.broadcasted_iota(jnp.int32, (kinds, width), 0).astype(jnp.float32)
    table = table_ref[...]
    second = second_ref[...]

    def layer_one(at):
        taps = jnp.concatenate([onehot_s[at - first_spread], onehot_s[at], onehot_s[at + first_spread]], axis=0)
        mixing = jnp.dot(table, jnp.concatenate([taps, taps], axis=0), preferred_element_type=jnp.float32)
        shifted = mixing[:channels]
        hidden = mixing[channels:] + jnp.maximum(shifted, jnp.exp2(jnp.minimum(shifted, SHIFT)) + (SHIFT - LOG2E))
        hidden_s[at] = hidden
        narrow_s[at] = hidden.astype(narrow_s.dtype)

    def layer_two(at):
        taps = jnp.concatenate([narrow_s[at - second_spread], narrow_s[at], narrow_s[at + second_spread]], axis=0)
        mixing = jnp.dot(second, taps, preferred_element_type=jnp.float32)
        return hidden_s[at] + jnp.maximum(mixing, LOG2E * jnp.exp2(jnp.minimum(mixing, 0.0)) - LOG2E)

    def run(first, count, emit, before, between, after):
        def hot(step, carry):
            block = token_s[pl.ds(pl.multiple_of(first + step * 8, 8), 8), :]
            for k in range(8):
                onehot_s[step * 8 + k] = jnp.where(block[k : k + 1, :] == letters, 1.0, 0.0).astype(onehot_s.dtype)
            return carry

        lax.fori_loop(0, (count + 2 * HALO) // 8, hot, 0)

        def clear(start):
            for k in range(DMAX):
                place = first - HALO + start + k

                @pl.when((place < 0) | (place >= length))
                def _():
                    narrow_s[start + k] = jnp.zeros((channels, width), narrow_s.dtype)

        ahead = BLOCK + 2 * DMAX
        for k in range(ahead):
            layer_one(DMAX + k)
        clear(DMAX)

        def trip(step, carry):
            before(step)
            between(step)
            for k in range(BLOCK):
                emit(step, k, layer_two(HALO + step * BLOCK + k))
                layer_one(DMAX + ahead + step * BLOCK + k)
            after(step)
            return carry

        last = count // BLOCK - 1
        lax.fori_loop(0, last, trip, 0)
        clear(count + HALO)
        before(last)
        between(last)
        for k in range(BLOCK):
            emit(last, k, layer_two(HALO + last * BLOCK + k))
        after(last)

    def emit_row(step, k, value):
        marks = mark_s[pl.ds(row_first + step * BLOCK + k, 1), :]
        row_ref[step * BLOCK + k] = (value * marks).astype(row_ref.dtype)

    def emit_col(step, k, value):
        for piece in range(width // lanes):
            turn_s[pl.ds(piece * channels * pitch + k, channels, stride=pitch), :] = value[
                :, piece * lanes : (piece + 1) * lanes
            ]

    def leave(step):
        slot = lax.rem(step, 2)
        start = pl.multiple_of(step * BLOCK, BLOCK)
        return pltpu.make_async_copy(stage_s.at[slot], col_ref.at[:, pl.ds(start, BLOCK), :], sems.at[slot])

    def await_stage(step):
        @pl.when(step >= 3)
        def _():
            leave(step - 3).wait()

    def turn_block(step):
        slot = lax.rem(step + 1, 2)
        start = pl.multiple_of(jnp.maximum(step - 1, 0) * BLOCK, BLOCK)
        marks = col_mark_ref[pl.ds(start, BLOCK), :]
        for channel in range(channels):
            for piece in range(width // lanes):
                part = slice(piece * lanes, (piece + 1) * lanes)
                place = (piece * channels + channel) * pitch
                stage_s[slot, channel, :, part] = turn_s[place : place + BLOCK, :].astype(stage_s.dtype) * marks[:, part]

    def send_block(step):
        @pl.when(step >= 1)
        def _():
            leave(step - 1).start()

    nothing = lambda step: None
    run(row_first, rows, emit_row, nothing, nothing, nothing)
    run(col_first, cols, emit_col, await_stage, turn_block, send_block)
    steps = cols // BLOCK
    if steps >= 3:
        leave(steps - 3).wait()
    turn_block(steps)
    leave(steps - 1).start()
    for step in range(max(steps - 2, 0), steps):
        leave(step).wait()


def features(dilations, here, there, table, second, rows, cols):
    blocks, _, each, length = here.shape
    width = 2 * blocks * each
    channels = second.shape[0]
    kinds = table.shape[1] // 6
    span = max(rows, cols) + 2 * HALO
    pitch = BLOCK + 8
    bf16, f32 = jnp.bfloat16, jnp.float32
    full = lambda shape: pl.BlockSpec(shape, functools.partial(lambda rank, g, s: (0,) * rank, len(shape)))
    return pl.pallas_call(
        functools.partial(feature_kernel, pitch=pitch),
        grid_spec=pltpu.PrefetchScalarGridSpec(
            num_scalar_prefetch=1,
            grid=(1,),
            in_specs=[full(x.shape) for x in (here, there, table, second)],
            out_specs=[
                full((rows, channels, width)),
                pl.BlockSpec(memory_space=pl.ANY),
                full((rows, width)),
                full((cols, width)),
            ],
            scratch_shapes=[
                pltpu.VMEM((length + 2 * HALO, width), f32),
                pltpu.VMEM((length, width), f32),
                pltpu.VMEM((span, kinds, width), bf16),
                pltpu.VMEM((span, channels, width), f32),
                pltpu.VMEM((span, channels, width), bf16),
                pltpu.VMEM((width // 128 * channels * pitch, 128), f32),
                pltpu.VMEM((2, channels, BLOCK, width), bf16),
                pltpu.SemaphoreType.DMA((2,)),
            ],
        ),
        out_shape=[
            jax.ShapeDtypeStruct((rows, channels, width), bf16),
            jax.ShapeDtypeStruct((channels, cols, width), bf16),
            jax.ShapeDtypeStruct((rows, width), bf16),
            jax.ShapeDtypeStruct((cols, width), bf16),
        ],
        compiler_params=pltpu.CompilerParams(vmem_limit_bytes=VMEM_LIMIT),
        cost_estimate=pl.CostEstimate(
            flops=40 * channels * channels * width * (rows + cols),
            bytes_accessed=2 * channels * width * (rows + cols),
            transcendentals=2 * channels * width * (rows + cols),
        ),
    )(dilations, here, there, table, second)


def outer_kernel(*refs, picks, halves, swap):
    count = len(picks)
    row_refs = refs[: halves * count]
    col_refs = refs[halves * count : halves * (count + 1)]
    projection_ref = refs[halves * (count + 1)]
    marks = refs[halves * (count + 1) + 1 : -(count + 2)]
    pair_refs = refs[-(count + 2) : -2]
    edge_ref, sum_s = refs[-2:]
    step = pl.program_id(0)
    group, cols, _ = col_refs[0].shape
    channels = row_refs[0].shape[1]
    rows = count * HALO

    @pl.when(step == 0)
    def _():
        sum_s[...] = jnp.zeros_like(sum_s)

    right = jnp.concatenate([ref[...].reshape(group * cols, ref.shape[2]) for ref in col_refs], axis=1)
    left = jnp.concatenate(
        [
            jnp.concatenate([row_refs[p * halves + h][...].reshape(HALO * channels, -1) for h in range(halves)], axis=1)
            for p in range(count)
        ],
        axis=0,
    )
    projection = projection_ref[...]
    outer = contract_last(left, right).astype(jnp.bfloat16)
    for pair in range(0, rows, 2):
        sides = [
            jnp.concatenate(
                [outer[i * channels : (i + 1) * channels, b * cols : (b + 1) * cols] for b in range(group)], axis=0
            )
            for i in (pair, pair + 1)
        ]
        sum_s[pair // 2] += jnp.dot(
            projection, jnp.concatenate(sides, axis=1), preferred_element_type=jnp.float32
        )

    @pl.when(step == pl.num_programs(0) - 1)
    def _():
        row_marks, col_marks = marks[:halves], marks[halves:]
        counts = sum(contract_last(r[...], c[...]) for r, c in zip(row_marks, col_marks))
        share = 1.0 / ((counts + 1.0) * (LOG2E * LOG2E))
        for p, pick in enumerate(picks):
            for k in range(HALO):
                i = p * HALO + k
                place = pick * HALO + k
                value = sum_s[i // 2][:, (i % 2) * cols : (i % 2 + 1) * cols] * share[place : place + 1, :]
                value = value.T
                pair_refs[p][k] = value.astype(edge_ref.dtype)
                if swap:
                    edge_ref[i] = jnp.where(lax.axis_index("col") == 0, value[cols - HALO :], value[:HALO]).astype(edge_ref.dtype)
        if not swap:
            edge_ref[...] = jnp.zeros_like(edge_ref)


def outer_products(row_feats, col_feats, projection, row_marks, col_marks, picks, swap, group=8):
    _, channels, _ = row_feats[0].shape
    cols = col_feats[0].shape[1]
    out = projection.shape[0]
    total = sum(x.shape[2] for x in row_feats)
    tall = len(picks) * HALO
    full = lambda shape: pl.BlockSpec(shape, functools.partial(lambda rank, g: (0,) * rank, len(shape)))
    picked = lambda pick, width: pl.BlockSpec((HALO, channels, width), lambda g: (pick, 0, 0))
    results = pl.pallas_call(
        functools.partial(outer_kernel, picks=picks, halves=len(row_feats), swap=swap),
        grid_spec=pl.GridSpec(
            grid=(channels // group,),
            in_specs=[picked(pick, x.shape[2]) for pick in picks for x in row_feats]
            + [pl.BlockSpec((group, cols, x.shape[2]), lambda g: (g, 0, 0)) for x in col_feats]
            + [pl.BlockSpec((out, group * channels), lambda g: (0, g))]
            + [full(x.shape) for x in (*row_marks, *col_marks)],
            out_specs=[full((HALO, cols, out)) for _ in picks] + [full((tall, HALO, out))],
            scratch_shapes=[pltpu.VMEM((tall // 2, out, 2 * cols), jnp.float32)],
        ),
        out_shape=[jax.ShapeDtypeStruct((HALO, cols, out), jnp.bfloat16) for _ in picks]
        + [jax.ShapeDtypeStruct((tall, HALO, out), jnp.bfloat16)],
        compiler_params=pltpu.CompilerParams(vmem_limit_bytes=VMEM_LIMIT),
        cost_estimate=pl.CostEstimate(
            flops=2 * tall * cols * channels * channels * (total + out),
            bytes_accessed=2 * channels * total * (tall + cols),
            transcendentals=0,
        ),
    )(
        *[x for _ in picks for x in row_feats],
        *col_feats,
        projection,
        *row_marks,
        *col_marks,
    )
    return list(results[:-1]), results[-1]


def conv_kernel(dilations, *refs, length, swap, rows, cols):
    first_spread, second_spread = dilations[NL1], dilations[NL1 + 1]
    row_first, col_first = lax.axis_index("row") * rows, lax.axis_index("col") * cols
    blocks = rows // HALO + 2
    row_refs = refs[:blocks]
    margin_refs = refs[blocks:-6]
    filter_ref, out_ref, wide_s, first_s, hidden_s, second_s = refs[-6:]
    channels = out_ref.shape[2]
    tall, pitch = rows + 2 * DMAX, cols + 2 * HALO
    f32, bf16 = jnp.float32, jnp.bfloat16
    for block, ref in enumerate(row_refs):
        for k in range(HALO):
            start = (block * HALO + k) * pitch + HALO
            wide_s[start : start + cols, :] = ref[k].astype(f32)
    for i in range(rows + 2 * HALO):
        if swap:
            edge = margin_refs[0][i].astype(f32)
            left = jnp.where(col_first == 0, jnp.zeros_like(edge), edge)
            right = jnp.where(col_first == 0, edge, jnp.zeros_like(edge))
        else:
            left, right = margin_refs[0][i].astype(f32), margin_refs[1][i].astype(f32)
        wide_s[i * pitch : i * pitch + HALO, :] = left
        wide_s[i * pitch + HALO + cols : (i + 1) * pitch, :] = right
    weights = [
        jnp.concatenate(
            [filter_ref[layer, k * channels : (k + 1) * channels, :].astype(f32).T for k in range(9)], axis=1
        ).astype(bf16)
        for layer in range(2)
    ]

    def spread_taps(source, target, count, spread, width, span):
        def body(i, carry):
            for tap in range(3):
                start = i * pitch + DMAX + (tap - 1) * spread
                for at in range(0, width, 16):
                    piece = source[pl.ds(start + at, 16), :].astype(bf16)
                    target[pl.ds(pl.multiple_of(i * span + at, 16), 16), tap * channels : (tap + 1) * channels] = piece
            return carry

        lax.fori_loop(0, count, body, 0, unroll=2)

    def mix(source, layer, start, spread, span):
        taps = jnp.concatenate(
            [
                source[pl.ds(pl.multiple_of(start + (DMAX + (tap - 1) * spread) * span, 16), TILE), :]
                for tap in range(3)
            ],
            axis=1,
        )
        return contract_last(weights[layer], taps)

    spread_taps(wide_s, first_s, rows + 2 * HALO, first_spread, pitch, pitch)

    def one(step, carry):
        start = pl.multiple_of(step * TILE, TILE)
        hidden_s[pl.ds(start, TILE), :] = elu(mix(first_s, 0, start, first_spread, pitch)).T
        return carry

    lax.fori_loop(0, -(-tall * pitch // TILE), one, 0, unroll=2)
    for i in range(tall):
        place = row_first - DMAX + i
        if i < DMAX or i >= tall - DMAX:

            @pl.when((place < 0) | (place >= length))
            def _():
                hidden_s[i * pitch : (i + 1) * pitch, :] = jnp.zeros((pitch, channels), f32)

    @pl.when(col_first == 0)
    def _():
        for i in range(tall):
            hidden_s[i * pitch : i * pitch + DMAX, :] = jnp.zeros((DMAX, channels), f32)

    @pl.when(col_first + cols == length)
    def _():
        for i in range(tall):
            start = i * pitch + DMAX + cols
            hidden_s[start : start + DMAX, :] = jnp.zeros((DMAX, channels), f32)

    spread_taps(hidden_s, second_s, tall, second_spread, cols, cols)

    def two(step, carry):
        start = pl.multiple_of(step * TILE, TILE)
        mixing = mix(second_s, 1, start, second_spread, cols).T
        for k in range(TILE // cols):
            i = step * (TILE // cols) + k
            own = wide_s[pl.ds(pl.multiple_of((i + HALO) * pitch + HALO, 8), cols), :]
            out_ref[i] = (own + mixing[k * cols : (k + 1) * cols]).astype(out_ref.dtype)
        return carry

    lax.fori_loop(0, rows * cols // TILE, two, 0, unroll=2)


def pair_convolutions(dilations, blocks, margins, filters, length, swap):
    cols, channels = blocks[0].shape[1:]
    rows = (len(blocks) - 2) * HALO
    pitch = cols + 2 * HALO
    padded = -(-(rows + 2 * DMAX) * pitch // TILE) * TILE
    operands = (*blocks, *margins, filters)
    full = lambda shape: pl.BlockSpec(shape, functools.partial(lambda rank, g, s: (0,) * rank, len(shape)))
    return pl.pallas_call(
        functools.partial(conv_kernel, length=length, swap=swap, rows=rows, cols=cols),
        grid_spec=pltpu.PrefetchScalarGridSpec(
            num_scalar_prefetch=1,
            grid=(1,),
            in_specs=[full(x.shape) for x in operands],
            out_specs=full((rows, cols, channels)),
            scratch_shapes=[
                pltpu.VMEM(((rows + 2 * HALO) * pitch + HALO, channels), jnp.float32),
                pltpu.VMEM((padded + 2 * DMAX * pitch, 3 * channels), jnp.bfloat16),
                pltpu.VMEM((padded, channels), jnp.float32),
                pltpu.VMEM(((rows + 2 * DMAX) * cols, 3 * channels), jnp.bfloat16),
            ],
        ),
        out_shape=jax.ShapeDtypeStruct((rows, cols, channels), jnp.bfloat16),
        compiler_params=pltpu.CompilerParams(vmem_limit_bytes=40 << 20),
    )(dilations, *operands)


def col_margins(tall):
    steps = range(lax.axis_size("col") - 1)
    head, tail = tall[:, :HALO], tall[:, tall.shape[1] - HALO :]
    return (
        lax.ppermute(tail, "col", [(i, i + 1) for i in steps]),
        lax.ppermute(head, "col", [(i + 1, i) for i in steps]),
    )


def per_device(tokens, gap_mask, dilations, embedding, residue_filters, projection, pair_filters):
    length = tokens.shape[1]
    row_count, col_count = lax.axis_size("row"), lax.axis_size("col")
    rows, cols = length // row_count, length // col_count
    col_index = lax.axis_index("col")
    swap = col_count == 2
    near = first_sequences(tokens, gap_mask)
    near_there = exchange(near, "col", 1)
    far = exchange(near, "row", row_count // 2)
    far_there = exchange(far, "col", 1)
    table, second, turned = prepare(embedding, residue_filters, projection)
    near_parts = features(dilations, near, near_there, table, second, rows, cols)
    far_parts = features(dilations, far, far_there, table, second, rows, cols)
    row_feats, col_feats, row_marks, col_marks = zip(near_parts, far_parts)
    last = rows // HALO - 1
    run = functools.partial(outer_products, row_feats, col_feats, turned, row_marks, col_marks, swap=swap)
    ends, end_edges = run(picks=(0, last))
    steps = range(row_count - 1)
    above = lax.ppermute(ends[1], "row", [(i, i + 1) for i in steps])
    below = lax.ppermute(ends[0], "row", [(i + 1, i) for i in steps])
    if last > 1:
        middle, middle_edges = run(picks=tuple(range(1, last)))
    else:
        middle, middle_edges = [], end_edges[:0]
    blocks = [above, ends[0], *middle, ends[1], below]
    if swap:
        pick = lambda block: jnp.where(col_index == 0, block[:, cols - HALO :], block[:, :HALO])
        edges = jnp.concatenate([pick(above), end_edges[:HALO], middle_edges, end_edges[HALO:], pick(below)])
        edges = exchange(edges, "col", 1)
        margins = [edges]
    else:
        margins = col_margins(jnp.concatenate(blocks))
    filters = pair_filters.reshape(2, 9 * pair_filters.shape[3], pair_filters.shape[4])
    return pair_convolutions(dilations, blocks, margins, filters, length, swap)


def solution(mesh):
    in_specs = (
        P(("grp", "row", "col"), None),
        P(("grp", "row", "col"), None),
        P(),
        P(),
        P(),
        P(),
        P(),
    )
    out_specs = P(("grp", "row"), "col", None)
    return jax.shard_map(per_device, mesh=mesh, in_specs=in_specs, out_specs=out_specs, check_vma=False)
```

```python
import functools
import math

import jax
import jax.numpy as jnp
from jax import lax
from jax.experimental import pallas as pl
from jax.experimental.pallas import tpu as pltpu
from jax.sharding import PartitionSpec as P


NL1 = 2
DMAX = 4
HALO = 2 * DMAX
BLOCK = 32
LANES = 128
LOG2E = 1.4426950408889634
SHIFT = math.log2(LOG2E)


def elu(x):
    return jnp.maximum(x, jnp.exp(jnp.minimum(x, 0.0)) - 1.0)


def contract_last(left, right):
    return lax.dot_general(
        left, right, (((1,), (1,)), ((), ())), preferred_element_type=jnp.float32
    )


def exchange(block, axis, bit):
    count = lax.axis_size(axis)
    return lax.ppermute(block, axis, [(i, i ^ bit) for i in range(count)])


def first_sequences(tokens, gap_mask):
    half = jnp.stack([tokens, gap_mask]).astype(jnp.bfloat16)[None]
    bit = lax.axis_size("row") // 4
    while bit >= 1:
        half = jnp.concatenate([half, exchange(half, "row", bit)])
        bit //= 2
    return half


def prepare_kernel(embedding_ref, filters_ref, projection_ref, table_ref, second_ref, turned_ref, letter_s, turn_s):
    letters, channels = embedding_ref.shape
    kinds = letter_s.shape[0]
    f32, bf16 = jnp.float32, jnp.bfloat16
    letter_s[...] = jnp.zeros_like(letter_s)
    letter_s[0:letters, :] = embedding_ref[...]
    letter = letter_s[...]
    for tap in range(3):
        mixed = LOG2E * lax.dot_general(
            filters_ref[0, tap], letter, (((1,), (1,)), ((), ())),
            precision=lax.Precision.HIGHEST, preferred_element_type=f32,
        )
        plain = jnp.zeros((channels, kinds), f32)
        if tap == 1:
            mixed = mixed + SHIFT
            plain = LOG2E * letter.T - SHIFT
        for first, value in ((0, mixed), (channels, plain)):
            high = value.astype(bf16)
            low = (value - high.astype(f32)).astype(bf16)
            for part, piece in enumerate((high, low)):
                start = (part * 3 + tap) * kinds
                table_ref[first : first + channels, start : start + kinds] = piece
        second_ref[:, tap * channels : (tap + 1) * channels] = filters_ref[1, tap].astype(bf16)
    pitch = turn_s.shape[0] // channels

    def widen(a, carry):
        start = pl.multiple_of(a * channels, channels)
        turn_s[pl.ds(pl.multiple_of(a * pitch, 8), channels), :] = projection_ref[pl.ds(start, channels), :].astype(f32)
        return carry

    lax.fori_loop(0, channels, widen, 0, unroll=4)

    def turn(step, carry):
        pair = jnp.concatenate([turn_s[pl.ds(2 * step + k, channels, stride=pitch), :] for k in range(2)], axis=0)
        start = pl.multiple_of(step * 2 * channels, 2 * channels)
        turned_ref[:, pl.ds(start, 2 * channels)] = pair.T.astype(bf16)
        return carry

    lax.fori_loop(0, channels // 2, turn, 0, unroll=2)


def prepare(embedding, filters, projection):
    letters, channels = embedding.shape
    kinds = -(-letters // 32) * 32
    out = projection.shape[1]
    bf16 = jnp.bfloat16
    return pl.pallas_call(
        prepare_kernel,
        out_shape=[
            jax.ShapeDtypeStruct((2 * channels, 6 * kinds), bf16),
            jax.ShapeDtypeStruct((channels, 3 * channels), bf16),
            jax.ShapeDtypeStruct((out, channels * channels), bf16),
        ],
        scratch_shapes=[
            pltpu.VMEM((kinds, channels), jnp.float32),
            pltpu.VMEM((channels * (channels + 8), out), jnp.float32),
        ],
        compiler_params=pltpu.CompilerParams(vmem_limit_bytes=62 << 20),
        cost_estimate=pl.CostEstimate(flops=10**6, bytes_accessed=4 << 20, transcendentals=0),
    )(embedding, filters, projection)


def feature_kernel(
    dilations, here_ref, there_ref, table_ref, second_ref, row_ref, col_ref, row_mark_ref, col_mark_ref,
    token_s, mark_s, onehot_s, hidden_s, narrow_s, turn_s, stage_s, sems, *, pitch,
):
    first_spread, second_spread = dilations[0], dilations[1]
    blocks, _, each, length = here_ref.shape
    part = blocks * each
    width = 2 * part
    channels = second_ref.shape[0]
    kinds = onehot_s.shape[1]
    rows, cols = row_ref.shape[0], col_ref.shape[1]
    row_first, col_first = lax.axis_index("row") * rows, lax.axis_index("col") * cols
    lanes = LANES
    for side, ref in enumerate((here_ref, there_ref)):
        at = slice(side * part, (side + 1) * part)
        token_s[HALO : HALO + length, at] = ref[:, 0].reshape(part, length).astype(jnp.float32).T
        mark_s[:, at] = ref[:, 1].reshape(part, length).astype(jnp.float32).T
    edge = jnp.full((HALO, width), -1.0, jnp.float32)
    token_s[0:HALO, :] = edge
    token_s[HALO + length : 2 * HALO + length, :] = edge
    row_mark_ref[...] = mark_s[pl.ds(pl.multiple_of(row_first, 8), rows), :].astype(row_mark_ref.dtype)
    col_mark_ref[...] = mark_s[pl.ds(pl.multiple_of(col_first, 8), cols), :].astype(col_mark_ref.dtype)
    letters = lax.broadcasted_iota(jnp.int32, (kinds, width), 0).astype(jnp.float32)
    table = table_ref[...]
    second = second_ref[...]

    def layer_one(at):
        taps = jnp.concatenate([onehot_s[at - first_spread], onehot_s[at], onehot_s[at + first_spread]], axis=0)
        mixing = jnp.dot(table, jnp.concatenate([taps, taps], axis=0), preferred_element_type=jnp.float32)
        shifted = mixing[:channels]
        hidden = mixing[channels:] + jnp.maximum(shifted, jnp.exp2(jnp.minimum(shifted, SHIFT)) + (SHIFT - LOG2E))
        hidden_s[at] = hidden
        narrow_s[at] = hidden.astype(narrow_s.dtype)

    def layer_two(at):
        taps = jnp.concatenate([narrow_s[at - second_spread], narrow_s[at], narrow_s[at + second_spread]], axis=0)
        mixing = jnp.dot(second, taps, preferred_element_type=jnp.float32)
        return hidden_s[at] + jnp.maximum(mixing, LOG2E * jnp.exp2(jnp.minimum(mixing, 0.0)) - LOG2E)

    def run(first, count, emit, before, between, after):
        block = min(BLOCK, count)

        def hot(step, carry):
            block = token_s[pl.ds(pl.multiple_of(first + step * 8, 8), 8), :]
            for k in range(8):
                onehot_s[step * 8 + k] = jnp.where(block[k : k + 1, :] == letters, 1.0, 0.0).astype(onehot_s.dtype)
            return carry

        lax.fori_loop(0, (count + 2 * HALO) // 8, hot, 0)

        def clear(start):
            for k in range(DMAX):
                place = first - HALO + start + k

                @pl.when((place < 0) | (place >= length))
                def _():
                    narrow_s[start + k] = jnp.zeros((channels, width), narrow_s.dtype)

        ahead = block + 2 * DMAX
        for k in range(ahead):
            layer_one(DMAX + k)
        clear(DMAX)

        def trip(step, carry):
            before(step)
            between(step)
            for k in range(block):
                emit(step, k, layer_two(HALO + step * block + k))
            for k in range(block):
                layer_one(DMAX + ahead + step * block + k)
            after(step)
            return carry

        last = count // block - 1
        lax.fori_loop(0, last, trip, 0)
        clear(count + HALO)
        before(last)
        between(last)
        for k in range(block):
            emit(last, k, layer_two(HALO + last * block + k))
        after(last)

    def emit_row(step, k, value):
        index = step * min(BLOCK, rows) + k
        marks = mark_s[pl.ds(row_first + index, 1), :]
        row_ref[index] = (value * marks).astype(row_ref.dtype)

    def emit_col(step, k, value):
        for piece in range(width // lanes):
            turn_s[pl.ds(piece * channels * pitch + k, channels, stride=pitch), :] = value[
                :, piece * lanes : (piece + 1) * lanes
            ]

    def leave(step):
        slot = lax.rem(step, 2)
        start = pl.multiple_of(step * BLOCK, BLOCK)
        return pltpu.make_async_copy(stage_s.at[slot], col_ref.at[:, pl.ds(start, BLOCK), :], sems.at[slot])

    def await_stage(step):
        @pl.when(step >= 3)
        def _():
            leave(step - 3).wait()

    def turn_block(step):
        slot = lax.rem(step + 1, 2)
        start = pl.multiple_of(jnp.maximum(step - 1, 0) * BLOCK, BLOCK)
        marks = mark_s[pl.ds(pl.multiple_of(col_first + start, 8), BLOCK), :]
        for channel in range(channels):
            for piece in range(width // lanes):
                part = slice(piece * lanes, (piece + 1) * lanes)
                place = (piece * channels + channel) * pitch
                stage_s[slot, channel, :, part] = (turn_s[place : place + BLOCK, :] * marks[:, part]).astype(stage_s.dtype)

    def send_block(step):
        @pl.when(step >= 1)
        def _():
            leave(step - 1).start()

    nothing = lambda step: None
    run(row_first, rows, emit_row, nothing, nothing, nothing)
    run(col_first, cols, emit_col, await_stage, turn_block, send_block)
    steps = cols // BLOCK
    if steps >= 3:
        leave(steps - 3).wait()
    turn_block(steps)
    leave(steps - 1).start()
    for step in range(max(steps - 2, 0), steps):
        leave(step).wait()


def features(dilations, here, there, table, second, rows, cols):
    blocks, _, each, length = here.shape
    width = 2 * blocks * each
    channels = second.shape[0]
    kinds = table.shape[1] // 6
    span = max(rows, cols) + 2 * HALO
    pitch = BLOCK + 1
    bf16, f32 = jnp.bfloat16, jnp.float32
    full = lambda shape: pl.BlockSpec(shape, functools.partial(lambda rank, g, s: (0,) * rank, len(shape)))
    return pl.pallas_call(
        functools.partial(feature_kernel, pitch=pitch),
        grid_spec=pltpu.PrefetchScalarGridSpec(
            num_scalar_prefetch=1,
            grid=(1,),
            in_specs=[full(x.shape) for x in (here, there, table, second)],
            out_specs=[
                full((rows, channels, width)),
                pl.BlockSpec(memory_space=pl.ANY),
                full((rows, width)),
                full((cols, width)),
            ],
            scratch_shapes=[
                pltpu.VMEM((length + 2 * HALO, width), f32),
                pltpu.VMEM((length, width), f32),
                pltpu.VMEM((span, kinds, width), bf16),
                pltpu.VMEM((span, channels, width), f32),
                pltpu.VMEM((span, channels, width), bf16),
                pltpu.VMEM((width // 128 * channels * pitch, 128), f32),
                pltpu.VMEM((2, channels, BLOCK, width), bf16),
                pltpu.SemaphoreType.DMA((2,)),
            ],
        ),
        out_shape=[
            jax.ShapeDtypeStruct((rows, channels, width), bf16),
            jax.ShapeDtypeStruct((channels, cols, width), bf16),
            jax.ShapeDtypeStruct((rows, width), bf16),
            jax.ShapeDtypeStruct((cols, width), bf16),
        ],
        compiler_params=pltpu.CompilerParams(vmem_limit_bytes=40 << 20),
        cost_estimate=pl.CostEstimate(
            flops=40 * channels * channels * width * (rows + cols),
            bytes_accessed=2 * channels * width * (rows + cols),
            transcendentals=2 * channels * width * (rows + cols),
        ),
    )(dilations, here, there, table, second)


def outer_kernel(*refs, picks, halves, swap):
    count = len(picks)
    row_refs = refs[: halves * count]
    col_refs = refs[halves * count : halves * (count + 1)]
    projection_ref = refs[halves * (count + 1)]
    marks = refs[halves * (count + 1) + 1 : -(count + 2)]
    pair_refs = refs[-(count + 2) : -2]
    edge_ref, sum_s = refs[-2:]
    step = pl.program_id(0)
    group, cols, _ = col_refs[0].shape
    channels = row_refs[0].shape[1]
    rows = count * HALO

    @pl.when(step == 0)
    def _():
        sum_s[...] = jnp.zeros_like(sum_s)

    right = jnp.concatenate([ref[...].reshape(group * cols, ref.shape[2]) for ref in col_refs], axis=1)
    left = jnp.concatenate(
        [
            jnp.concatenate([row_refs[p * halves + h][...].reshape(HALO * channels, -1) for h in range(halves)], axis=1)
            for p in range(count)
        ],
        axis=0,
    )
    projection = projection_ref[...]
    outer = contract_last(left, right).astype(jnp.bfloat16)
    for pair in range(0, rows, 2):
        sides = [
            jnp.concatenate(
                [outer[i * channels : (i + 1) * channels, b * cols : (b + 1) * cols] for b in range(group)], axis=0
            )
            for i in (pair, pair + 1)
        ]
        sum_s[pair // 2] += jnp.dot(
            projection, jnp.concatenate(sides, axis=1), preferred_element_type=jnp.float32
        )

    @pl.when(step == pl.num_programs(0) - 1)
    def _():
        row_marks, col_marks = marks[:halves], marks[halves:]
        counts = sum(contract_last(r[...], c[...]) for r, c in zip(row_marks, col_marks))
        share = 1.0 / ((counts + 1.0) * (LOG2E * LOG2E))
        for p, pick in enumerate(picks):
            for k in range(HALO):
                i = p * HALO + k
                place = pick * HALO + k
                value = sum_s[i // 2][:, (i % 2) * cols : (i % 2 + 1) * cols] * share[place : place + 1, :]
                value = value.T
                pair_refs[p][k] = value.astype(edge_ref.dtype)
                if swap:
                    edge_ref[i] = jnp.where(lax.axis_index("col") == 0, value[cols - HALO :], value[:HALO]).astype(edge_ref.dtype)
        if not swap:
            edge_ref[...] = jnp.zeros_like(edge_ref)


def outer_products(row_feats, col_feats, projection, row_marks, col_marks, picks, swap, group=8):
    _, channels, _ = row_feats[0].shape
    cols = col_feats[0].shape[1]
    out = projection.shape[0]
    total = sum(x.shape[2] for x in row_feats)
    tall = len(picks) * HALO
    full = lambda shape: pl.BlockSpec(shape, functools.partial(lambda rank, g: (0,) * rank, len(shape)))
    picked = lambda pick, width: pl.BlockSpec((HALO, channels, width), lambda g: (pick, 0, 0))
    results = pl.pallas_call(
        functools.partial(outer_kernel, picks=picks, halves=len(row_feats), swap=swap),
        grid_spec=pl.GridSpec(
            grid=(channels // group,),
            in_specs=[picked(pick, x.shape[2]) for pick in picks for x in row_feats]
            + [pl.BlockSpec((group, cols, x.shape[2]), lambda g: (g, 0, 0)) for x in col_feats]
            + [pl.BlockSpec((out, group * channels), lambda g: (0, g))]
            + [full(x.shape) for x in (*row_marks, *col_marks)],
            out_specs=[full((HALO, cols, out)) for _ in picks] + [full((tall, HALO, out))],
            scratch_shapes=[pltpu.VMEM((tall // 2, out, 2 * cols), jnp.float32)],
        ),
        out_shape=[jax.ShapeDtypeStruct((HALO, cols, out), jnp.bfloat16) for _ in picks]
        + [jax.ShapeDtypeStruct((tall, HALO, out), jnp.bfloat16)],
        compiler_params=pltpu.CompilerParams(vmem_limit_bytes=32 << 20),
        cost_estimate=pl.CostEstimate(
            flops=2 * tall * cols * channels * channels * (total + out),
            bytes_accessed=2 * channels * total * (tall + cols),
            transcendentals=0,
        ),
    )(
        *[x for _ in picks for x in row_feats],
        *col_feats,
        projection,
        *row_marks,
        *col_marks,
    )
    return list(results[:-1]), results[-1]


def conv_kernel(dilations, *refs, length, swap, rows, cols):
    first_spread, second_spread = dilations[NL1], dilations[NL1 + 1]
    row_first, col_first = lax.axis_index("row") * rows, lax.axis_index("col") * cols
    blocks = rows // HALO + 2
    row_refs = refs[:blocks]
    margin_refs = refs[blocks:-9]
    filter_ref, out_ref, wide_s, first_s, hidden_s, second_s, weight_s, out_s, sem = refs[-9:]
    channels = out_ref.shape[2]
    tall, pitch = rows + 2 * DMAX, cols + 2 * HALO
    f32, bf16 = jnp.float32, jnp.bfloat16
    for block, ref in enumerate(row_refs):
        for k in range(HALO):
            start = (block * HALO + k) * pitch + HALO
            wide_s[start : start + cols, :] = ref[k].astype(f32)
    for i in range(rows + 2 * HALO):
        if swap:
            edge = margin_refs[0][i].astype(f32)
            left = jnp.where(col_first == 0, jnp.zeros_like(edge), edge)
            right = jnp.where(col_first == 0, edge, jnp.zeros_like(edge))
        else:
            left, right = margin_refs[0][i].astype(f32), margin_refs[1][i].astype(f32)
        wide_s[i * pitch : i * pitch + HALO, :] = left
        wide_s[i * pitch + HALO + cols : (i + 1) * pitch, :] = right
    for layer in range(2):
        deep = 3 * channels
        weight_s[layer, 3 * deep :, 0:channels] = jnp.zeros((deep, channels), bf16)
        weight_s[layer, :deep, channels:] = jnp.zeros((deep, channels), bf16)
        weight_s[layer, : 3 * deep, 0:channels] = filter_ref[layer]
        weight_s[layer, deep:, channels:] = filter_ref[layer]

    def spread_taps(source, target, count, spread, width, span):
        def body(i, carry):
            for tap in range(3):
                start = i * pitch + DMAX + (tap - 1) * spread
                for at in range(0, width, 16):
                    piece = source[pl.ds(start + at, 16), :].astype(bf16)
                    target[pl.ds(pl.multiple_of(i * span + at, 16), 16), tap * channels : (tap + 1) * channels] = piece
            return carry

        lax.fori_loop(0, count, body, 0, unroll=2)

    for target, count, span in ((first_s, rows + 2 * HALO, pitch), (second_s, tall, cols)):
        target[count * span : (count + DMAX) * span, :] = jnp.zeros((DMAX * span, 3 * channels), bf16)

    def mix(source, layer, pair, spread, span):
        first = 2 * spread * lax.div(pair, spread) + lax.rem(pair, spread)
        taps = jnp.concatenate(
            [
                source[pl.ds(pl.multiple_of((first + DMAX + (tap - 1) * spread) * span, 16), span), :]
                for tap in range(4)
            ],
            axis=1,
        )
        mixing = jnp.dot(taps, weight_s[layer], preferred_element_type=f32)
        return (first, mixing[:, :channels]), (first + spread, mixing[:, channels:])

    spread_taps(wide_s, first_s, rows + 2 * HALO, first_spread, pitch, pitch)

    def one(pair, carry):
        for i, mixing in mix(first_s, 0, pair, first_spread, pitch):
            hidden_s[pl.ds(pl.multiple_of(i * pitch, 8), pitch), :] = elu(mixing)
        return carry

    lax.fori_loop(0, row_pairs(tall), one, 0, unroll=3)
    for i in range(tall):
        place = row_first - DMAX + i
        if i < DMAX or i >= tall - DMAX:

            @pl.when((place < 0) | (place >= length))
            def _():
                hidden_s[i * pitch : (i + 1) * pitch, :] = jnp.zeros((pitch, channels), f32)

    @pl.when(col_first == 0)
    def _():
        for i in range(tall):
            hidden_s[i * pitch : i * pitch + DMAX, :] = jnp.zeros((DMAX, channels), f32)

    @pl.when(col_first + cols == length)
    def _():
        for i in range(tall):
            start = i * pitch + DMAX + cols
            hidden_s[start : start + DMAX, :] = jnp.zeros((DMAX, channels), f32)

    spread_taps(hidden_s, second_s, tall, second_spread, cols, cols)

    def two(pair, carry):
        for i, mixing in mix(second_s, 1, pair, second_spread, cols):
            own = wide_s[pl.ds(pl.multiple_of(jnp.minimum(i + HALO, rows + 2 * HALO - 1) * pitch + HALO, 8), cols), :]
            out_s[i] = (own + mixing).astype(out_s.dtype)
        return carry

    lax.fori_loop(0, row_pairs(rows), two, 0, unroll=3)
    copy = pltpu.make_async_copy(out_s.at[0:rows], out_ref, sem)
    copy.start()
    copy.wait()


def row_pairs(count):
    return max(d * -(-count // (2 * d)) for d in range(1, DMAX + 1))


def pair_convolutions(dilations, blocks, margins, filters, length, swap):
    cols, channels = blocks[0].shape[1:]
    rows = (len(blocks) - 2) * HALO
    pitch = cols + 2 * HALO
    tall = rows + 2 * DMAX
    operands = (*blocks, *margins, filters)
    full = lambda shape: pl.BlockSpec(shape, functools.partial(lambda rank, g, s: (0,) * rank, len(shape)))
    return pl.pallas_call(
        functools.partial(conv_kernel, length=length, swap=swap, rows=rows, cols=cols),
        grid_spec=pltpu.PrefetchScalarGridSpec(
            num_scalar_prefetch=1,
            grid=(1,),
            in_specs=[full(x.shape) for x in operands],
            out_specs=pl.BlockSpec(memory_space=pl.ANY),
            scratch_shapes=[
                pltpu.VMEM(((rows + 2 * HALO) * pitch + HALO, channels), jnp.float32),
                pltpu.VMEM(((tall + 4 * DMAX) * pitch, 3 * channels), jnp.bfloat16),
                pltpu.VMEM(((tall + 2 * DMAX) * pitch, channels), jnp.float32),
                pltpu.VMEM(((rows + 4 * DMAX) * cols, 3 * channels), jnp.bfloat16),
                pltpu.VMEM((2, 12 * channels, 2 * channels), jnp.bfloat16),
                pltpu.VMEM((rows + 2 * DMAX, cols, channels), jnp.bfloat16),
                pltpu.SemaphoreType.DMA,
            ],
        ),
        out_shape=jax.ShapeDtypeStruct((rows, cols, channels), jnp.bfloat16),
        compiler_params=pltpu.CompilerParams(vmem_limit_bytes=40 << 20),
    )(dilations, *operands)


def col_margins(tall):
    steps = range(lax.axis_size("col") - 1)
    head, tail = tall[:, :HALO], tall[:, tall.shape[1] - HALO :]
    return (
        lax.ppermute(tail, "col", [(i, i + 1) for i in steps]),
        lax.ppermute(head, "col", [(i + 1, i) for i in steps]),
    )


def per_device(tokens, gap_mask, dilations, embedding, residue_filters, projection, pair_filters):
    length = tokens.shape[1]
    row_count, col_count = lax.axis_size("row"), lax.axis_size("col")
    rows, cols = length // row_count, length // col_count
    col_index = lax.axis_index("col")
    swap = col_count == 2
    near = first_sequences(tokens, gap_mask)
    near_there = exchange(near, "col", 1)
    far = exchange(near, "row", row_count // 2)
    far_there = exchange(near_there, "row", row_count // 2)
    table, second, turned = prepare(embedding, residue_filters, projection)
    near_parts = features(dilations, near, near_there, table, second, rows, cols)
    far_parts = features(dilations, far, far_there, table, second, rows, cols)
    row_feats, col_feats, row_marks, col_marks = zip(near_parts, far_parts)
    last = rows // HALO - 1
    run = functools.partial(outer_products, row_feats, col_feats, turned, row_marks, col_marks, swap=swap)
    ends, end_edges = run(picks=(0, last))
    steps = range(row_count - 1)
    above = lax.ppermute(ends[1], "row", [(i, i + 1) for i in steps])
    below = lax.ppermute(ends[0], "row", [(i + 1, i) for i in steps])
    if last > 1:
        middle, middle_edges = run(picks=tuple(range(1, last)))
    else:
        middle, middle_edges = [], end_edges[:0]
    blocks = [above, ends[0], *middle, ends[1], below]
    if swap:
        pick = lambda block: jnp.where(col_index == 0, block[:, cols - HALO :], block[:, :HALO])
        edges = jnp.concatenate([pick(above), end_edges[:HALO], middle_edges, end_edges[HALO:], pick(below)])
        edges = exchange(edges, "col", 1)
        margins = [edges]
    else:
        margins = col_margins(jnp.concatenate(blocks))
    filters = pair_filters.reshape(2, 9 * pair_filters.shape[3], pair_filters.shape[4])
    return pair_convolutions(dilations, blocks, margins, filters, length, swap)


def solution(mesh):
    in_specs = (
        P(("grp", "row", "col"), None),
        P(("grp", "row", "col"), None),
        P(),
        P(),
        P(),
        P(),
        P(),
    )
    out_specs = P(("grp", "row"), "col", None)
    return jax.shard_map(per_device, mesh=mesh, in_specs=in_specs, out_specs=out_specs, check_vma=False)
```

```python
import functools
import math

import jax
import jax.numpy as jnp
from jax import lax
from jax.experimental import pallas as pl
from jax.experimental.pallas import tpu as pltpu
from jax.sharding import PartitionSpec as P


NL1 = 2
DMAX = 4
HALO = 2 * DMAX
BLOCK = 32
LANES = 128
LOG2E = 1.4426950408889634
SHIFT = math.log2(LOG2E)


def elu(x):
    return jnp.maximum(x, jnp.exp(jnp.minimum(x, 0.0)) - 1.0)


def in_hbm(array):
    return pltpu.with_memory_space_constraint(array, pltpu.HBM)


def contract_last(left, right):
    return lax.dot_general(
        left, right, (((1,), (1,)), ((), ())), preferred_element_type=jnp.float32
    )


def exchange(block, axis, bit):
    count = lax.axis_size(axis)
    return lax.ppermute(block, axis, [(i, i ^ bit) for i in range(count)])


def first_sequences(tokens, gap_mask):
    half = jnp.stack([tokens, gap_mask]).astype(jnp.bfloat16)[None]
    bit = lax.axis_size("row") // 4
    while bit >= 1:
        half = jnp.concatenate([half, exchange(half, "row", bit)])
        bit //= 2
    return half


def prepare_kernel(embedding_ref, filters_ref, table_ref, second_ref, letter_s):
    letters, channels = embedding_ref.shape
    kinds = letter_s.shape[0]
    f32, bf16 = jnp.float32, jnp.bfloat16
    letter_s[...] = jnp.zeros_like(letter_s)
    letter_s[0:letters, :] = embedding_ref[...]
    letter = letter_s[...]
    for tap in range(3):
        mixed = LOG2E * lax.dot_general(
            filters_ref[0, tap], letter, (((1,), (1,)), ((), ())),
            precision=lax.Precision.HIGHEST, preferred_element_type=f32,
        )
        plain = jnp.zeros((channels, kinds), f32)
        if tap == 1:
            mixed = mixed + SHIFT
            plain = LOG2E * letter.T - SHIFT
        for first, value in ((0, mixed), (channels, plain)):
            high = value.astype(bf16)
            low = (value - high.astype(f32)).astype(bf16)
            for part, piece in enumerate((high, low)):
                start = (part * 3 + tap) * kinds
                table_ref[first : first + channels, start : start + kinds] = piece
        second_ref[:, tap * channels : (tap + 1) * channels] = filters_ref[1, tap].astype(bf16)


def prepare(embedding, filters):
    letters, channels = embedding.shape
    kinds = -(-letters // 32) * 32
    bf16 = jnp.bfloat16
    return pl.pallas_call(
        prepare_kernel,
        out_shape=[
            jax.ShapeDtypeStruct((2 * channels, 6 * kinds), bf16),
            jax.ShapeDtypeStruct((channels, 3 * channels), bf16),
        ],
        scratch_shapes=[
            pltpu.VMEM((kinds, channels), jnp.float32),
        ],
        compiler_params=pltpu.CompilerParams(vmem_limit_bytes=62 << 20),
        cost_estimate=pl.CostEstimate(flops=10**6, bytes_accessed=1 << 18, transcendentals=0),
    )(in_hbm(embedding), in_hbm(filters))


def feature_kernel(
    dilations, here_ref, there_ref, table_ref, second_ref, row_ref, col_ref, row_mark_ref, col_mark_ref,
    token_s, mark_s, onehot_s, hidden_s, narrow_s, turn_s, stage_s, sems, *, pitch,
):
    first_spread, second_spread = dilations[0], dilations[1]
    blocks, _, each, length = here_ref.shape
    part = blocks * each
    width = 2 * part
    channels = second_ref.shape[0]
    kinds = onehot_s.shape[1]
    rows, cols = row_ref.shape[0], col_ref.shape[1]
    row_first, col_first = lax.axis_index("row") * rows, lax.axis_index("col") * cols
    lanes = LANES
    for side, ref in enumerate((here_ref, there_ref)):
        at = slice(side * part, (side + 1) * part)
        token_s[HALO : HALO + length, at] = ref[:, 0].reshape(part, length).astype(jnp.float32).T
        mark_s[:, at] = ref[:, 1].reshape(part, length).astype(jnp.float32).T
    edge = jnp.full((HALO, width), -1.0, jnp.float32)
    token_s[0:HALO, :] = edge
    token_s[HALO + length : 2 * HALO + length, :] = edge
    row_mark_ref[...] = mark_s[pl.ds(pl.multiple_of(row_first, 8), rows), :].astype(row_mark_ref.dtype)
    col_mark_ref[...] = mark_s[pl.ds(pl.multiple_of(col_first, 8), cols), :].astype(col_mark_ref.dtype)
    letters = lax.broadcasted_iota(jnp.int32, (kinds, width), 0).astype(jnp.float32)
    table = table_ref[...]
    second = second_ref[...]

    def layer_one(at):
        taps = jnp.concatenate([onehot_s[at - first_spread], onehot_s[at], onehot_s[at + first_spread]], axis=0)
        mixing = jnp.dot(table, jnp.concatenate([taps, taps], axis=0), preferred_element_type=jnp.float32)
        shifted = mixing[:channels]
        hidden = mixing[channels:] + jnp.maximum(shifted, jnp.exp2(jnp.minimum(shifted, SHIFT)) + (SHIFT - LOG2E))
        hidden_s[at] = hidden
        narrow_s[at] = hidden.astype(narrow_s.dtype)

    def layer_two(at):
        taps = jnp.concatenate([narrow_s[at - second_spread], narrow_s[at], narrow_s[at + second_spread]], axis=0)
        mixing = jnp.dot(second, taps, preferred_element_type=jnp.float32)
        return hidden_s[at] + jnp.maximum(mixing, LOG2E * jnp.exp2(jnp.minimum(mixing, 0.0)) - LOG2E)

    def run(first, count, emit, before, between, after):
        block = min(BLOCK, count)

        def hot(step, carry):
            block = token_s[pl.ds(pl.multiple_of(first + step * 8, 8), 8), :]
            for k in range(8):
                onehot_s[step * 8 + k] = jnp.where(block[k : k + 1, :] == letters, 1.0, 0.0).astype(onehot_s.dtype)
            return carry

        lax.fori_loop(0, (count + 2 * HALO) // 8, hot, 0)

        def clear(start):
            for k in range(DMAX):
                place = first - HALO + start + k

                @pl.when((place < 0) | (place >= length))
                def _():
                    narrow_s[start + k] = jnp.zeros((channels, width), narrow_s.dtype)

        ahead = block + 2 * DMAX
        for k in range(ahead):
            layer_one(DMAX + k)
        clear(DMAX)

        def trip(step, carry):
            before(step)
            between(step)
            for k in range(block):
                emit(step, k, layer_two(HALO + step * block + k))
            for k in range(block):
                layer_one(DMAX + ahead + step * block + k)
            after(step)
            return carry

        last = count // block - 1
        lax.fori_loop(0, last, trip, 0)
        clear(count + HALO)
        before(last)
        between(last)
        for k in range(block):
            emit(last, k, layer_two(HALO + last * block + k))
        after(last)

    def emit_row(step, k, value):
        index = step * min(BLOCK, rows) + k
        marks = mark_s[pl.ds(row_first + index, 1), :]
        row_ref[index] = (value * marks).astype(row_ref.dtype)

    def emit_col(step, k, value):
        for piece in range(width // lanes):
            turn_s[pl.ds(piece * channels * pitch + k, channels, stride=pitch), :] = value[
                :, piece * lanes : (piece + 1) * lanes
            ]

    def leave(step):
        slot = lax.rem(step, 2)
        start = pl.multiple_of(step * BLOCK, BLOCK)
        return pltpu.make_async_copy(stage_s.at[slot], col_ref.at[:, pl.ds(start, BLOCK), :], sems.at[slot])

    def await_stage(step):
        @pl.when(step >= 3)
        def _():
            leave(step - 3).wait()

    def turn_block(step):
        slot = lax.rem(step + 1, 2)
        start = pl.multiple_of(jnp.maximum(step - 1, 0) * BLOCK, BLOCK)
        marks = mark_s[pl.ds(pl.multiple_of(col_first + start, 8), BLOCK), :]
        for channel in range(channels):
            for piece in range(width // lanes):
                part = slice(piece * lanes, (piece + 1) * lanes)
                place = (piece * channels + channel) * pitch
                stage_s[slot, channel, :, part] = (turn_s[place : place + BLOCK, :] * marks[:, part]).astype(stage_s.dtype)

    def send_block(step):
        @pl.when(step >= 1)
        def _():
            leave(step - 1).start()

    nothing = lambda step: None
    run(row_first, rows, emit_row, nothing, nothing, nothing)
    run(col_first, cols, emit_col, await_stage, turn_block, send_block)
    steps = cols // BLOCK
    if steps >= 3:
        leave(steps - 3).wait()
    turn_block(steps)
    leave(steps - 1).start()
    for step in range(max(steps - 2, 0), steps):
        leave(step).wait()


def features(dilations, here, there, table, second, rows, cols):
    blocks, _, each, length = here.shape
    width = 2 * blocks * each
    channels = second.shape[0]
    kinds = table.shape[1] // 6
    span = max(rows, cols) + 2 * HALO
    pitch = BLOCK + 1
    bf16, f32 = jnp.bfloat16, jnp.float32
    full = lambda shape: pl.BlockSpec(shape, functools.partial(lambda rank, g, s: (0,) * rank, len(shape)))
    return pl.pallas_call(
        functools.partial(feature_kernel, pitch=pitch),
        grid_spec=pltpu.PrefetchScalarGridSpec(
            num_scalar_prefetch=1,
            grid=(1,),
            in_specs=[full(x.shape) for x in (here, there, table, second)],
            out_specs=[
                full((rows, channels, width)),
                pl.BlockSpec(memory_space=pl.ANY),
                full((rows, width)),
                full((cols, width)),
            ],
            scratch_shapes=[
                pltpu.VMEM((length + 2 * HALO, width), f32),
                pltpu.VMEM((length, width), f32),
                pltpu.VMEM((span, kinds, width), bf16),
                pltpu.VMEM((span, channels, width), f32),
                pltpu.VMEM((span, channels, width), bf16),
                pltpu.VMEM((width // 128 * channels * pitch, 128), f32),
                pltpu.VMEM((2, channels, BLOCK, width), bf16),
                pltpu.SemaphoreType.DMA((2,)),
            ],
        ),
        out_shape=[
            jax.ShapeDtypeStruct((rows, channels, width), bf16),
            jax.ShapeDtypeStruct((channels, cols, width), bf16),
            jax.ShapeDtypeStruct((rows, width), bf16),
            jax.ShapeDtypeStruct((cols, width), bf16),
        ],
        compiler_params=pltpu.CompilerParams(vmem_limit_bytes=40 << 20),
        cost_estimate=pl.CostEstimate(
            flops=40 * channels * channels * width * (rows + cols),
            bytes_accessed=2 * channels * width * (rows + cols),
            transcendentals=2 * channels * width * (rows + cols),
        ),
    )(in_hbm(dilations), here, there, in_hbm(table), in_hbm(second))


def outer_kernel(*refs, picks, halves, swap):
    count = len(picks)
    row_refs = refs[: halves * count]
    col_refs = refs[halves * count : halves * (count + 1)]
    projection_ref = refs[halves * (count + 1)]
    marks = refs[halves * (count + 1) + 1 : -(count + 3)]
    pair_refs = refs[-(count + 3) : -3]
    edge_ref, sum_s, turn_s = refs[-3:]
    step = pl.program_id(0)
    group, cols, _ = col_refs[0].shape
    channels = row_refs[0].shape[1]
    rows = count * HALO

    @pl.when(step == 0)
    def _():
        sum_s[...] = jnp.zeros_like(sum_s)

    right = jnp.concatenate([ref[...].reshape(group * cols, ref.shape[2]) for ref in col_refs], axis=1)
    left = jnp.concatenate(
        [
            jnp.concatenate([row_refs[p * halves + h][...].reshape(HALO * channels, -1) for h in range(halves)], axis=1)
            for p in range(count)
        ],
        axis=0,
    )
    pitch = turn_s.shape[0] // channels
    for a in range(channels):
        turn_s[a * pitch : a * pitch + group, :] = projection_ref[a].astype(jnp.float32)
    turned = []
    for b in range(0, group, 2):
        pair = jnp.concatenate([turn_s[pl.ds(b + k, channels, stride=pitch), :] for k in range(2)], axis=0)
        turned.append(pair.T.astype(jnp.bfloat16))
    projection = jnp.concatenate(turned, axis=1)
    outer = contract_last(left, right).astype(jnp.bfloat16)
    for pair in range(0, rows, 2):
        sides = [
            jnp.concatenate(
                [outer[i * channels : (i + 1) * channels, b * cols : (b + 1) * cols] for b in range(group)], axis=0
            )
            for i in (pair, pair + 1)
        ]
        sum_s[pair // 2] += jnp.dot(
            projection, jnp.concatenate(sides, axis=1), preferred_element_type=jnp.float32
        )

    @pl.when(step == pl.num_programs(0) - 1)
    def _():
        row_marks, col_marks = marks[:halves], marks[halves:]
        counts = sum(contract_last(r[...], c[...]) for r, c in zip(row_marks, col_marks))
        share = 1.0 / ((counts + 1.0) * (LOG2E * LOG2E))
        for p, pick in enumerate(picks):
            for k in range(HALO):
                i = p * HALO + k
                place = pick * HALO + k
                value = sum_s[i // 2][:, (i % 2) * cols : (i % 2 + 1) * cols] * share[place : place + 1, :]
                value = value.T
                pair_refs[p][k] = value.astype(edge_ref.dtype)
                if swap:
                    edge_ref[i] = jnp.where(lax.axis_index("col") == 0, value[cols - HALO :], value[:HALO]).astype(edge_ref.dtype)
        if not swap:
            edge_ref[...] = jnp.zeros_like(edge_ref)


def outer_products(row_feats, col_feats, projection, row_marks, col_marks, picks, swap, group=8):
    _, channels, _ = row_feats[0].shape
    cols = col_feats[0].shape[1]
    out = projection.shape[2]
    total = sum(x.shape[2] for x in row_feats)
    tall = len(picks) * HALO
    full = lambda shape: pl.BlockSpec(shape, functools.partial(lambda rank, g: (0,) * rank, len(shape)))
    picked = lambda pick, width: pl.BlockSpec((HALO, channels, width), lambda g: (pick, 0, 0))
    results = pl.pallas_call(
        functools.partial(outer_kernel, picks=picks, halves=len(row_feats), swap=swap),
        grid_spec=pl.GridSpec(
            grid=(channels // group,),
            in_specs=[picked(pick, x.shape[2]) for pick in picks for x in row_feats]
            + [pl.BlockSpec((group, cols, x.shape[2]), lambda g: (g, 0, 0)) for x in col_feats]
            + [pl.BlockSpec((channels, group, out), lambda g: (0, g, 0))]
            + [full(x.shape) for x in (*row_marks, *col_marks)],
            out_specs=[full((HALO, cols, out)) for _ in picks] + [full((tall, HALO, out))],
            scratch_shapes=[
                pltpu.VMEM((tall // 2, out, 2 * cols), jnp.float32),
                pltpu.VMEM((channels * (group + 1), out), jnp.float32),
            ],
        ),
        out_shape=[jax.ShapeDtypeStruct((HALO, cols, out), jnp.bfloat16) for _ in picks]
        + [jax.ShapeDtypeStruct((tall, HALO, out), jnp.bfloat16)],
        compiler_params=pltpu.CompilerParams(vmem_limit_bytes=32 << 20),
        cost_estimate=pl.CostEstimate(
            flops=2 * tall * cols * channels * channels * (total + out),
            bytes_accessed=2 * channels * total * (tall + cols),
            transcendentals=0,
        ),
    )(
        *[x for _ in picks for x in row_feats],
        *col_feats,
        projection,
        *row_marks,
        *col_marks,
    )
    return list(results[:-1]), results[-1]


def conv_kernel(dilations, *refs, length, swap, rows, cols):
    first_spread, second_spread = dilations[NL1], dilations[NL1 + 1]
    row_first, col_first = lax.axis_index("row") * rows, lax.axis_index("col") * cols
    blocks = rows // HALO + 2
    row_refs = refs[:blocks]
    margin_refs = refs[blocks:-9]
    filter_ref, out_ref, wide_s, first_s, hidden_s, second_s, weight_s, out_s, sem = refs[-9:]
    channels = out_ref.shape[2]
    tall, pitch = rows + 2 * DMAX, cols + 2 * HALO
    f32, bf16 = jnp.float32, jnp.bfloat16
    for block, ref in enumerate(row_refs):
        for k in range(HALO):
            start = (block * HALO + k) * pitch + HALO
            wide_s[start : start + cols, :] = ref[k].astype(f32)
    for i in range(rows + 2 * HALO):
        if swap:
            edge = margin_refs[0][i].astype(f32)
            left = jnp.where(col_first == 0, jnp.zeros_like(edge), edge)
            right = jnp.where(col_first == 0, edge, jnp.zeros_like(edge))
        else:
            left, right = margin_refs[0][i].astype(f32), margin_refs[1][i].astype(f32)
        wide_s[i * pitch : i * pitch + HALO, :] = left
        wide_s[i * pitch + HALO + cols : (i + 1) * pitch, :] = right
    for layer in range(2):
        deep = 3 * channels
        weight_s[layer, 3 * deep :, 0:channels] = jnp.zeros((deep, channels), bf16)
        weight_s[layer, :deep, channels:] = jnp.zeros((deep, channels), bf16)
        weight_s[layer, : 3 * deep, 0:channels] = filter_ref[layer]
        weight_s[layer, deep:, channels:] = filter_ref[layer]

    def spread_taps(source, target, count, spread, width, span):
        def body(i, carry):
            for tap in range(3):
                start = i * pitch + DMAX + (tap - 1) * spread
                for at in range(0, width, 16):
                    piece = source[pl.ds(start + at, 16), :].astype(bf16)
                    target[pl.ds(pl.multiple_of(i * span + at, 16), 16), tap * channels : (tap + 1) * channels] = piece
            return carry

        lax.fori_loop(0, count, body, 0, unroll=2)

    for target, count, span in ((first_s, rows + 2 * HALO, pitch), (second_s, tall, cols)):
        target[count * span : (count + DMAX) * span, :] = jnp.zeros((DMAX * span, 3 * channels), bf16)

    def mix(source, layer, pair, spread, span):
        first = 2 * spread * lax.div(pair, spread) + lax.rem(pair, spread)
        taps = jnp.concatenate(
            [
                source[pl.ds(pl.multiple_of((first + DMAX + (tap - 1) * spread) * span, 16), span), :]
                for tap in range(4)
            ],
            axis=1,
        )
        mixing = jnp.dot(taps, weight_s[layer], preferred_element_type=f32)
        return (first, mixing[:, :channels]), (first + spread, mixing[:, channels:])

    spread_taps(wide_s, first_s, rows + 2 * HALO, first_spread, pitch, pitch)

    def one(pair, carry):
        for i, mixing in mix(first_s, 0, pair, first_spread, pitch):
            hidden_s[pl.ds(pl.multiple_of(i * pitch, 8), pitch), :] = elu(mixing)
        return carry

    lax.fori_loop(0, row_pairs(tall), one, 0, unroll=3)
    for i in range(tall):
        place = row_first - DMAX + i
        if i < DMAX or i >= tall - DMAX:

            @pl.when((place < 0) | (place >= length))
            def _():
                hidden_s[i * pitch : (i + 1) * pitch, :] = jnp.zeros((pitch, channels), f32)

    @pl.when(col_first == 0)
    def _():
        for i in range(tall):
            hidden_s[i * pitch : i * pitch + DMAX, :] = jnp.zeros((DMAX, channels), f32)

    @pl.when(col_first + cols == length)
    def _():
        for i in range(tall):
            start = i * pitch + DMAX + cols
            hidden_s[start : start + DMAX, :] = jnp.zeros((DMAX, channels), f32)

    spread_taps(hidden_s, second_s, tall, second_spread, cols, cols)

    def two(pair, carry):
        for i, mixing in mix(second_s, 1, pair, second_spread, cols):
            own = wide_s[pl.ds(pl.multiple_of(jnp.minimum(i + HALO, rows + 2 * HALO - 1) * pitch + HALO, 8), cols), :]
            out_s[i] = (own + mixing).astype(out_s.dtype)
        return carry

    lax.fori_loop(0, row_pairs(rows), two, 0, unroll=3)
    copy = pltpu.make_async_copy(out_s.at[0:rows], out_ref, sem)
    copy.start()
    copy.wait()


def row_pairs(count):
    return max(d * -(-count // (2 * d)) for d in range(1, DMAX + 1))


def pair_convolutions(dilations, blocks, margins, filters, length, swap):
    cols, channels = blocks[0].shape[1:]
    rows = (len(blocks) - 2) * HALO
    pitch = cols + 2 * HALO
    tall = rows + 2 * DMAX
    operands = (*blocks, *margins, filters)
    full = lambda shape: pl.BlockSpec(shape, functools.partial(lambda rank, g, s: (0,) * rank, len(shape)))
    return pl.pallas_call(
        functools.partial(conv_kernel, length=length, swap=swap, rows=rows, cols=cols),
        grid_spec=pltpu.PrefetchScalarGridSpec(
            num_scalar_prefetch=1,
            grid=(1,),
            in_specs=[full(x.shape) for x in operands],
            out_specs=pl.BlockSpec(memory_space=pl.ANY),
            scratch_shapes=[
                pltpu.VMEM(((rows + 2 * HALO) * pitch + HALO, channels), jnp.float32),
                pltpu.VMEM(((tall + 4 * DMAX) * pitch, 3 * channels), jnp.bfloat16),
                pltpu.VMEM(((tall + 2 * DMAX) * pitch, channels), jnp.float32),
                pltpu.VMEM(((rows + 4 * DMAX) * cols, 3 * channels), jnp.bfloat16),
                pltpu.VMEM((2, 12 * channels, 2 * channels), jnp.bfloat16),
                pltpu.VMEM((rows + 2 * DMAX, cols, channels), jnp.bfloat16),
                pltpu.SemaphoreType.DMA,
            ],
        ),
        out_shape=jax.ShapeDtypeStruct((rows, cols, channels), jnp.bfloat16),
        compiler_params=pltpu.CompilerParams(vmem_limit_bytes=40 << 20),
    )(in_hbm(dilations), *operands)


def col_margins(tall):
    steps = range(lax.axis_size("col") - 1)
    head, tail = tall[:, :HALO], tall[:, tall.shape[1] - HALO :]
    return (
        lax.ppermute(tail, "col", [(i, i + 1) for i in steps]),
        lax.ppermute(head, "col", [(i + 1, i) for i in steps]),
    )


def per_device(tokens, gap_mask, dilations, embedding, residue_filters, projection, pair_filters):
    length = tokens.shape[1]
    row_count, col_count = lax.axis_size("row"), lax.axis_size("col")
    rows, cols = length // row_count, length // col_count
    col_index = lax.axis_index("col")
    swap = col_count == 2
    near = first_sequences(tokens, gap_mask)
    near_there = exchange(near, "col", 1)
    far = exchange(near, "row", row_count // 2)
    far_there = exchange(near_there, "row", row_count // 2)
    table, second = prepare(embedding, residue_filters)
    channels = embedding.shape[1]
    blocks = projection.reshape(channels, channels, projection.shape[1])
    near_parts = features(dilations, near, near_there, table, second, rows, cols)
    far_parts = features(dilations, far, far_there, table, second, rows, cols)
    row_feats, col_feats, row_marks, col_marks = zip(near_parts, far_parts)
    last = rows // HALO - 1
    run = functools.partial(outer_products, row_feats, col_feats, blocks, row_marks, col_marks, swap=swap)
    ends, end_edges = run(picks=(0, last))
    steps = range(row_count - 1)
    above = lax.ppermute(ends[1], "row", [(i, i + 1) for i in steps])
    below = lax.ppermute(ends[0], "row", [(i + 1, i) for i in steps])
    if last > 1:
        middle, middle_edges = run(picks=tuple(range(1, last)))
    else:
        middle, middle_edges = [], end_edges[:0]
    blocks = [above, ends[0], *middle, ends[1], below]
    if swap:
        pick = lambda block: jnp.where(col_index == 0, block[:, cols - HALO :], block[:, :HALO])
        edges = jnp.concatenate([pick(above), end_edges[:HALO], middle_edges, end_edges[HALO:], pick(below)])
        edges = exchange(edges, "col", 1)
        margins = [edges]
    else:
        margins = col_margins(jnp.concatenate(blocks))
    filters = pair_filters.reshape(2, 9 * pair_filters.shape[3], pair_filters.shape[4])
    return pair_convolutions(dilations, blocks, margins, filters, length, swap)


def solution(mesh):
    in_specs = (
        P(("grp", "row", "col"), None),
        P(("grp", "row", "col"), None),
        P(),
        P(),
        P(),
        P(),
        P(),
    )
    out_specs = P(("grp", "row"), "col", None)
    return jax.shard_map(per_device, mesh=mesh, in_specs=in_specs, out_specs=out_specs, check_vma=False)
```

```python
import functools
import math

import jax
import jax.numpy as jnp
from jax import lax
from jax.experimental import pallas as pl
from jax.experimental.pallas import tpu as pltpu
from jax.sharding import PartitionSpec as P


NL1 = 2
DMAX = 4
HALO = 2 * DMAX
BLOCK = 32
LANES = 128
LOG2E = 1.4426950408889634
SHIFT = math.log2(LOG2E)


def elu(x):
    return jnp.maximum(x, jnp.exp(jnp.minimum(x, 0.0)) - 1.0)


def in_hbm(array):
    return pltpu.with_memory_space_constraint(array, pltpu.HBM)


def contract_last(left, right):
    return lax.dot_general(
        left, right, (((1,), (1,)), ((), ())), preferred_element_type=jnp.float32
    )


def exchange(block, axis, bit):
    count = lax.axis_size(axis)
    return lax.ppermute(block, axis, [(i, i ^ bit) for i in range(count)])


def first_sequences(tokens, gap_mask):
    half = jnp.stack([tokens, gap_mask]).astype(jnp.bfloat16)[None]
    bit = lax.axis_size("row") // 4
    while bit >= 1:
        half = jnp.concatenate([half, exchange(half, "row", bit)])
        bit //= 2
    return half


def prepare_kernel(embedding_ref, filters_ref, table_ref, second_ref, letter_s):
    letters, channels = embedding_ref.shape
    kinds = letter_s.shape[0]
    f32, bf16 = jnp.float32, jnp.bfloat16
    letter_s[...] = jnp.zeros_like(letter_s)
    letter_s[0:letters, :] = embedding_ref[...]
    letter = letter_s[...]
    for tap in range(3):
        mixed = LOG2E * lax.dot_general(
            filters_ref[0, tap], letter, (((1,), (1,)), ((), ())),
            precision=lax.Precision.HIGHEST, preferred_element_type=f32,
        )
        plain = jnp.zeros((channels, kinds), f32)
        if tap == 1:
            mixed = mixed + SHIFT
            plain = LOG2E * letter.T - SHIFT
        for first, value in ((0, mixed), (channels, plain)):
            high = value.astype(bf16)
            low = (value - high.astype(f32)).astype(bf16)
            for part, piece in enumerate((high, low)):
                start = (part * 3 + tap) * kinds
                table_ref[first : first + channels, start : start + kinds] = piece
        second_ref[:, tap * channels : (tap + 1) * channels] = filters_ref[1, tap].astype(bf16)


def prepare(embedding, filters):
    letters, channels = embedding.shape
    kinds = -(-letters // 32) * 32
    bf16 = jnp.bfloat16
    return pl.pallas_call(
        prepare_kernel,
        out_shape=[
            jax.ShapeDtypeStruct((2 * channels, 6 * kinds), bf16),
            jax.ShapeDtypeStruct((channels, 3 * channels), bf16),
        ],
        scratch_shapes=[
            pltpu.VMEM((kinds, channels), jnp.float32),
        ],
        compiler_params=pltpu.CompilerParams(vmem_limit_bytes=16 << 20),
        cost_estimate=pl.CostEstimate(flops=10**6, bytes_accessed=1 << 18, transcendentals=0),
    )(in_hbm(embedding), in_hbm(filters))


def feature_kernel(
    dilations, here_ref, there_ref, table_ref, second_ref, row_ref, col_ref, row_mark_ref, col_mark_ref,
    token_s, mark_s, onehot_s, hidden_s, narrow_s, turn_s, stage_s, sems, *, pitch,
):
    first_spread, second_spread = dilations[0], dilations[1]
    blocks, _, each, length = here_ref.shape
    part = blocks * each
    width = 2 * part
    channels = second_ref.shape[0]
    kinds = onehot_s.shape[1]
    rows, cols = row_ref.shape[0], col_ref.shape[1]
    row_first, col_first = lax.axis_index("row") * rows, lax.axis_index("col") * cols
    lanes = LANES
    for side, ref in enumerate((here_ref, there_ref)):
        at = slice(side * part, (side + 1) * part)
        token_s[HALO : HALO + length, at] = ref[:, 0].reshape(part, length).astype(jnp.float32).T
        mark_s[:, at] = ref[:, 1].reshape(part, length).astype(jnp.float32).T
    edge = jnp.full((HALO, width), -1.0, jnp.float32)
    token_s[0:HALO, :] = edge
    token_s[HALO + length : 2 * HALO + length, :] = edge
    row_mark_ref[...] = mark_s[pl.ds(pl.multiple_of(row_first, 8), rows), :].astype(row_mark_ref.dtype)
    col_mark_ref[...] = mark_s[pl.ds(pl.multiple_of(col_first, 8), cols), :].astype(col_mark_ref.dtype)
    letters = lax.broadcasted_iota(jnp.int32, (kinds, width), 0).astype(jnp.float32)
    table = table_ref[...]
    second = second_ref[...]

    def layer_one(at):
        taps = jnp.concatenate([onehot_s[at - first_spread], onehot_s[at], onehot_s[at + first_spread]], axis=0)
        mixing = jnp.dot(table, jnp.concatenate([taps, taps], axis=0), preferred_element_type=jnp.float32)
        shifted = mixing[:channels]
        hidden = mixing[channels:] + jnp.maximum(shifted, jnp.exp2(jnp.minimum(shifted, SHIFT)) + (SHIFT - LOG2E))
        hidden_s[at] = hidden
        narrow_s[at] = hidden.astype(narrow_s.dtype)

    def layer_two(at):
        taps = jnp.concatenate([narrow_s[at - second_spread], narrow_s[at], narrow_s[at + second_spread]], axis=0)
        mixing = jnp.dot(second, taps, preferred_element_type=jnp.float32)
        return hidden_s[at] + jnp.maximum(mixing, LOG2E * jnp.exp2(jnp.minimum(mixing, 0.0)) - LOG2E)

    def run(first, count, emit, before, between, after):
        block = min(BLOCK, count)

        def hot(step, carry):
            block = token_s[pl.ds(pl.multiple_of(first + step * 8, 8), 8), :]
            for k in range(8):
                onehot_s[step * 8 + k] = jnp.where(block[k : k + 1, :] == letters, 1.0, 0.0).astype(onehot_s.dtype)
            return carry

        lax.fori_loop(0, (count + 2 * HALO) // 8, hot, 0)

        def clear(start):
            for k in range(DMAX):
                place = first - HALO + start + k

                @pl.when((place < 0) | (place >= length))
                def _():
                    narrow_s[start + k] = jnp.zeros((channels, width), narrow_s.dtype)

        ahead = block + 2 * DMAX
        for k in range(ahead):
            layer_one(DMAX + k)
        clear(DMAX)

        def trip(step, carry):
            before(step)
            between(step)
            for k in range(block):
                emit(step, k, layer_two(HALO + step * block + k))
            for k in range(block):
                layer_one(DMAX + ahead + step * block + k)
            after(step)
            return carry

        last = count // block - 1
        lax.fori_loop(0, last, trip, 0)
        clear(count + HALO)
        before(last)
        between(last)
        for k in range(block):
            emit(last, k, layer_two(HALO + last * block + k))
        after(last)

    def emit_row(step, k, value):
        index = step * min(BLOCK, rows) + k
        marks = mark_s[pl.ds(row_first + index, 1), :]
        row_ref[index] = (value * marks).astype(row_ref.dtype)

    def emit_col(step, k, value):
        for piece in range(width // lanes):
            turn_s[pl.ds(piece * channels * pitch + k, channels, stride=pitch), :] = value[
                :, piece * lanes : (piece + 1) * lanes
            ]

    def leave(step):
        slot = lax.rem(step, 2)
        start = pl.multiple_of(step * BLOCK, BLOCK)
        return pltpu.make_async_copy(stage_s.at[slot], col_ref.at[:, pl.ds(start, BLOCK), :], sems.at[slot])

    def await_stage(step):
        @pl.when(step >= 3)
        def _():
            leave(step - 3).wait()

    def turn_block(step):
        slot = lax.rem(step + 1, 2)
        start = pl.multiple_of(jnp.maximum(step - 1, 0) * BLOCK, BLOCK)
        marks = mark_s[pl.ds(pl.multiple_of(col_first + start, 8), BLOCK), :]
        for channel in range(channels):
            for piece in range(width // lanes):
                part = slice(piece * lanes, (piece + 1) * lanes)
                place = (piece * channels + channel) * pitch
                stage_s[slot, channel, :, part] = (turn_s[place : place + BLOCK, :] * marks[:, part]).astype(stage_s.dtype)

    def send_block(step):
        @pl.when(step >= 1)
        def _():
            leave(step - 1).start()

    nothing = lambda step: None
    run(row_first, rows, emit_row, nothing, nothing, nothing)
    run(col_first, cols, emit_col, await_stage, turn_block, send_block)
    steps = cols // BLOCK
    if steps >= 3:
        leave(steps - 3).wait()
    turn_block(steps)
    leave(steps - 1).start()
    for step in range(max(steps - 2, 0), steps):
        leave(step).wait()


def features(dilations, sequences, table, second, rows, cols):
    blocks, _, each, length = sequences.shape
    width = blocks * each
    side = (blocks // 2, 2, each, length)
    channels = second.shape[0]
    kinds = table.shape[1] // 6
    span = max(rows, cols) + 2 * HALO
    pitch = BLOCK + 1
    bf16, f32 = jnp.bfloat16, jnp.float32
    full = lambda shape: pl.BlockSpec(shape, functools.partial(lambda rank, g, s: (0,) * rank, len(shape)))
    return pl.pallas_call(
        functools.partial(feature_kernel, pitch=pitch),
        grid_spec=pltpu.PrefetchScalarGridSpec(
            num_scalar_prefetch=1,
            grid=(1,),
            in_specs=[pl.BlockSpec(side, lambda g, s: (0, 0, 0, 0)), pl.BlockSpec(side, lambda g, s: (1, 0, 0, 0))]
            + [full(x.shape) for x in (table, second)],
            out_specs=[
                full((rows, channels, width)),
                pl.BlockSpec(memory_space=pl.ANY),
                full((rows, width)),
                full((cols, width)),
            ],
            scratch_shapes=[
                pltpu.VMEM((length + 2 * HALO, width), f32),
                pltpu.VMEM((length, width), f32),
                pltpu.VMEM((span, kinds, width), bf16),
                pltpu.VMEM((span, channels, width), f32),
                pltpu.VMEM((span, channels, width), bf16),
                pltpu.VMEM((width // 128 * channels * pitch, 128), f32),
                pltpu.VMEM((2, channels, BLOCK, width), bf16),
                pltpu.SemaphoreType.DMA((2,)),
            ],
        ),
        out_shape=[
            jax.ShapeDtypeStruct((rows, channels, width), bf16),
            jax.ShapeDtypeStruct((channels, cols, width), bf16),
            jax.ShapeDtypeStruct((rows, width), bf16),
            jax.ShapeDtypeStruct((cols, width), bf16),
        ],
        compiler_params=pltpu.CompilerParams(vmem_limit_bytes=40 << 20),
        cost_estimate=pl.CostEstimate(
            flops=40 * channels * channels * width * (rows + cols),
            bytes_accessed=2 * channels * width * (rows + cols),
            transcendentals=2 * channels * width * (rows + cols),
        ),
    )(dilations, sequences, sequences, table, second)


def outer_kernel(*refs, picks, halves, swap):
    count = len(picks)
    row_refs = refs[: halves * count]
    col_refs = refs[halves * count : halves * (count + 1)]
    projection_ref = refs[halves * (count + 1)]
    marks = refs[halves * (count + 1) + 1 : -(count + 3)]
    pair_refs = refs[-(count + 3) : -3]
    edge_ref, sum_s, turn_s = refs[-3:]
    step = pl.program_id(0)
    group, cols, _ = col_refs[0].shape
    channels = row_refs[0].shape[1]
    rows = count * HALO

    @pl.when(step == 0)
    def _():
        sum_s[...] = jnp.zeros_like(sum_s)

    right = jnp.concatenate([ref[...].reshape(group * cols, ref.shape[2]) for ref in col_refs], axis=1)
    left = jnp.concatenate(
        [
            jnp.concatenate([row_refs[p * halves + h][...].reshape(HALO * channels, -1) for h in range(halves)], axis=1)
            for p in range(count)
        ],
        axis=0,
    )
    pitch = turn_s.shape[0] // channels
    for a in range(channels):
        turn_s[a * pitch : a * pitch + group, :] = projection_ref[a].astype(jnp.float32)
    turned = []
    for b in range(0, group, 2):
        pair = jnp.concatenate([turn_s[pl.ds(b + k, channels, stride=pitch), :] for k in range(2)], axis=0)
        turned.append(pair.T.astype(jnp.bfloat16))
    projection = jnp.concatenate(turned, axis=1)
    outer = contract_last(left, right).astype(jnp.bfloat16)
    for pair in range(0, rows, 2):
        sides = [
            jnp.concatenate(
                [outer[i * channels : (i + 1) * channels, b * cols : (b + 1) * cols] for b in range(group)], axis=0
            )
            for i in (pair, pair + 1)
        ]
        sum_s[pair // 2] += jnp.dot(
            projection, jnp.concatenate(sides, axis=1), preferred_element_type=jnp.float32
        )

    @pl.when(step == pl.num_programs(0) - 1)
    def _():
        row_marks, col_marks = marks[:halves], marks[halves:]
        counts = sum(contract_last(r[...], c[...]) for r, c in zip(row_marks, col_marks))
        share = 1.0 / ((counts + 1.0) * (LOG2E * LOG2E))
        for p, pick in enumerate(picks):
            for k in range(HALO):
                i = p * HALO + k
                place = pick * HALO + k
                value = sum_s[i // 2][:, (i % 2) * cols : (i % 2 + 1) * cols] * share[place : place + 1, :]
                value = value.T
                pair_refs[p][k] = value.astype(edge_ref.dtype)
                if swap:
                    edge_ref[i] = jnp.where(lax.axis_index("col") == 0, value[cols - HALO :], value[:HALO]).astype(edge_ref.dtype)
        if not swap:
            edge_ref[...] = jnp.zeros_like(edge_ref)


def outer_products(row_feats, col_feats, projection, row_marks, col_marks, picks, swap, group=8):
    _, channels, _ = row_feats[0].shape
    cols = col_feats[0].shape[1]
    out = projection.shape[2]
    total = sum(x.shape[2] for x in row_feats)
    tall = len(picks) * HALO
    full = lambda shape: pl.BlockSpec(shape, functools.partial(lambda rank, g: (0,) * rank, len(shape)))
    picked = lambda pick, width: pl.BlockSpec((HALO, channels, width), lambda g: (pick, 0, 0))
    results = pl.pallas_call(
        functools.partial(outer_kernel, picks=picks, halves=len(row_feats), swap=swap),
        grid_spec=pl.GridSpec(
            grid=(channels // group,),
            in_specs=[picked(pick, x.shape[2]) for pick in picks for x in row_feats]
            + [pl.BlockSpec((group, cols, x.shape[2]), lambda g: (g, 0, 0)) for x in col_feats]
            + [pl.BlockSpec((channels, group, out), lambda g: (0, g, 0))]
            + [full(x.shape) for x in (*row_marks, *col_marks)],
            out_specs=[full((HALO, cols, out)) for _ in picks] + [full((tall, HALO, out))],
            scratch_shapes=[
                pltpu.VMEM((tall // 2, out, 2 * cols), jnp.float32),
                pltpu.VMEM((channels * (group + 1), out), jnp.float32),
            ],
        ),
        out_shape=[jax.ShapeDtypeStruct((HALO, cols, out), jnp.bfloat16) for _ in picks]
        + [jax.ShapeDtypeStruct((tall, HALO, out), jnp.bfloat16)],
        compiler_params=pltpu.CompilerParams(vmem_limit_bytes=32 << 20),
        cost_estimate=pl.CostEstimate(
            flops=2 * tall * cols * channels * channels * (total + out),
            bytes_accessed=2 * channels * total * (tall + cols),
            transcendentals=0,
        ),
    )(
        *[x for _ in picks for x in row_feats],
        *col_feats,
        projection,
        *row_marks,
        *col_marks,
    )
    return list(results[:-1]), results[-1]


def conv_kernel(dilations, *refs, length, swap, rows, cols):
    first_spread, second_spread = dilations[NL1], dilations[NL1 + 1]
    row_first, col_first = lax.axis_index("row") * rows, lax.axis_index("col") * cols
    blocks = rows // HALO + 2
    row_refs = refs[:blocks]
    margin_refs = refs[blocks:-9]
    filter_ref, out_ref, wide_s, first_s, hidden_s, second_s, weight_s, out_s, sem = refs[-9:]
    channels = out_ref.shape[2]
    tall, pitch = rows + 2 * DMAX, cols + 2 * HALO
    f32, bf16 = jnp.float32, jnp.bfloat16
    for block, ref in enumerate(row_refs):
        for k in range(HALO):
            start = (block * HALO + k) * pitch + HALO
            wide_s[start : start + cols, :] = ref[k].astype(f32)
    for i in range(rows + 2 * HALO):
        if swap:
            edge = margin_refs[0][i].astype(f32)
            left = jnp.where(col_first == 0, jnp.zeros_like(edge), edge)
            right = jnp.where(col_first == 0, edge, jnp.zeros_like(edge))
        else:
            left, right = margin_refs[0][i].astype(f32), margin_refs[1][i].astype(f32)
        wide_s[i * pitch : i * pitch + HALO, :] = left
        wide_s[i * pitch + HALO + cols : (i + 1) * pitch, :] = right
    for layer in range(2):
        deep = 3 * channels
        weight_s[layer, 3 * deep :, 0:channels] = jnp.zeros((deep, channels), bf16)
        weight_s[layer, :deep, channels:] = jnp.zeros((deep, channels), bf16)
        weight_s[layer, : 3 * deep, 0:channels] = filter_ref[layer]
        weight_s[layer, deep:, channels:] = filter_ref[layer]

    def spread_taps(source, target, count, spread, width, span):
        def body(i, carry):
            for tap in range(3):
                start = i * pitch + DMAX + (tap - 1) * spread
                for at in range(0, width, 16):
                    piece = source[pl.ds(start + at, 16), :].astype(bf16)
                    target[pl.ds(pl.multiple_of(i * span + at, 16), 16), tap * channels : (tap + 1) * channels] = piece
            return carry

        lax.fori_loop(0, count, body, 0, unroll=2)

    for target, count, span in ((first_s, rows + 2 * HALO, pitch), (second_s, tall, cols)):
        target[count * span : (count + DMAX) * span, :] = jnp.zeros((DMAX * span, 3 * channels), bf16)

    def mix(source, layer, pair, spread, span):
        first = 2 * spread * lax.div(pair, spread) + lax.rem(pair, spread)
        taps = jnp.concatenate(
            [
                source[pl.ds(pl.multiple_of((first + DMAX + (tap - 1) * spread) * span, 16), span), :]
                for tap in range(4)
            ],
            axis=1,
        )
        mixing = jnp.dot(taps, weight_s[layer], preferred_element_type=f32)
        return (first, mixing[:, :channels]), (first + spread, mixing[:, channels:])

    spread_taps(wide_s, first_s, rows + 2 * HALO, first_spread, pitch, pitch)

    def one(pair, carry):
        for i, mixing in mix(first_s, 0, pair, first_spread, pitch):
            hidden_s[pl.ds(pl.multiple_of(i * pitch, 8), pitch), :] = elu(mixing)
        return carry

    lax.fori_loop(0, row_pairs(tall), one, 0, unroll=3)
    for i in range(tall):
        place = row_first - DMAX + i
        if i < DMAX or i >= tall - DMAX:

            @pl.when((place < 0) | (place >= length))
            def _():
                hidden_s[i * pitch : (i + 1) * pitch, :] = jnp.zeros((pitch, channels), f32)

    @pl.when(col_first == 0)
    def _():
        for i in range(tall):
            hidden_s[i * pitch : i * pitch + DMAX, :] = jnp.zeros((DMAX, channels), f32)

    @pl.when(col_first + cols == length)
    def _():
        for i in range(tall):
            start = i * pitch + DMAX + cols
            hidden_s[start : start + DMAX, :] = jnp.zeros((DMAX, channels), f32)

    spread_taps(hidden_s, second_s, tall, second_spread, cols, cols)

    def two(pair, carry):
        for i, mixing in mix(second_s, 1, pair, second_spread, cols):
            own = wide_s[pl.ds(pl.multiple_of(jnp.minimum(i + HALO, rows + 2 * HALO - 1) * pitch + HALO, 8), cols), :]
            out_s[i] = (own + mixing).astype(out_s.dtype)
        return carry

    lax.fori_loop(0, row_pairs(rows), two, 0, unroll=3)
    copy = pltpu.make_async_copy(out_s.at[0:rows], out_ref, sem)
    copy.start()
    copy.wait()


def row_pairs(count):
    return max(d * -(-count // (2 * d)) for d in range(1, DMAX + 1))


def pair_convolutions(dilations, blocks, margins, filters, length, swap):
    cols, channels = blocks[0].shape[1:]
    rows = (len(blocks) - 2) * HALO
    pitch = cols + 2 * HALO
    tall = rows + 2 * DMAX
    operands = (*blocks, *margins, filters)
    full = lambda shape: pl.BlockSpec(shape, functools.partial(lambda rank, g, s: (0,) * rank, len(shape)))
    return pl.pallas_call(
        functools.partial(conv_kernel, length=length, swap=swap, rows=rows, cols=cols),
        grid_spec=pltpu.PrefetchScalarGridSpec(
            num_scalar_prefetch=1,
            grid=(1,),
            in_specs=[full(x.shape) for x in operands],
            out_specs=pl.BlockSpec(memory_space=pl.ANY),
            scratch_shapes=[
                pltpu.VMEM(((rows + 2 * HALO) * pitch + HALO, channels), jnp.float32),
                pltpu.VMEM(((tall + 4 * DMAX) * pitch, 3 * channels), jnp.bfloat16),
                pltpu.VMEM(((tall + 2 * DMAX) * pitch, channels), jnp.float32),
                pltpu.VMEM(((rows + 4 * DMAX) * cols, 3 * channels), jnp.bfloat16),
                pltpu.VMEM((2, 12 * channels, 2 * channels), jnp.bfloat16),
                pltpu.VMEM((rows + 2 * DMAX, cols, channels), jnp.bfloat16),
                pltpu.SemaphoreType.DMA,
            ],
        ),
        out_shape=jax.ShapeDtypeStruct((rows, cols, channels), jnp.bfloat16),
        compiler_params=pltpu.CompilerParams(vmem_limit_bytes=40 << 20),
    )(dilations, *operands)


def col_margins(tall):
    steps = range(lax.axis_size("col") - 1)
    head, tail = tall[:, :HALO], tall[:, tall.shape[1] - HALO :]
    return (
        lax.ppermute(tail, "col", [(i, i + 1) for i in steps]),
        lax.ppermute(head, "col", [(i + 1, i) for i in steps]),
    )


def per_device(tokens, gap_mask, dilations, embedding, residue_filters, projection, pair_filters):
    length = tokens.shape[1]
    row_count, col_count = lax.axis_size("row"), lax.axis_size("col")
    rows, cols = length // row_count, length // col_count
    col_index = lax.axis_index("col")
    swap = col_count == 2
    near = first_sequences(tokens, gap_mask)
    near_there = exchange(near, "col", 1)
    near_both = jnp.concatenate([near, near_there])
    far_both = exchange(near_both, "row", row_count // 2)
    table, second = prepare(embedding, residue_filters)
    channels = embedding.shape[1]
    blocks = projection.reshape(channels, channels, projection.shape[1])
    near_parts = features(dilations, near_both, table, second, rows, cols)
    far_parts = features(dilations, far_both, table, second, rows, cols)
    row_feats, col_feats, row_marks, col_marks = zip(near_parts, far_parts)
    last = rows // HALO - 1
    run = functools.partial(outer_products, row_feats, col_feats, blocks, row_marks, col_marks, swap=swap)
    ends, end_edges = run(picks=(0, last))
    steps = range(row_count - 1)
    above = lax.ppermute(ends[1], "row", [(i, i + 1) for i in steps])
    below = lax.ppermute(ends[0], "row", [(i + 1, i) for i in steps])
    if last > 1:
        middle, middle_edges = run(picks=tuple(range(1, last)))
    else:
        middle, middle_edges = [], end_edges[:0]
    blocks = [above, ends[0], *middle, ends[1], below]
    if swap:
        pick = lambda block: jnp.where(col_index == 0, block[:, cols - HALO :], block[:, :HALO])
        edges = jnp.concatenate([pick(above), end_edges[:HALO], middle_edges, end_edges[HALO:], pick(below)])
        edges = exchange(edges, "col", 1)
        margins = [edges]
    else:
        margins = col_margins(jnp.concatenate(blocks))
    filters = pair_filters.reshape(2, 9 * pair_filters.shape[3], pair_filters.shape[4])
    return pair_convolutions(dilations, blocks, margins, filters, length, swap)


def solution(mesh):
    in_specs = (
        P(("grp", "row", "col"), None),
        P(("grp", "row", "col"), None),
        P(),
        P(),
        P(),
        P(),
        P(),
    )
    out_specs = P(("grp", "row"), "col", None)
    return jax.shard_map(per_device, mesh=mesh, in_specs=in_specs, out_specs=out_specs, check_vma=False)
```

```python
import functools
import math

import jax
import jax.numpy as jnp
from jax import lax
from jax.experimental import pallas as pl
from jax.experimental.pallas import tpu as pltpu
from jax.sharding import PartitionSpec as P


NL1 = 2
DMAX = 4
HALO = 2 * DMAX
BLOCK = 32
LANES = 128
LOG2E = 1.4426950408889634
SHIFT = math.log2(LOG2E)


def elu(x):
    return jnp.maximum(x, jnp.exp(jnp.minimum(x, 0.0)) - 1.0)


def in_hbm(array):
    return pltpu.with_memory_space_constraint(array, pltpu.HBM)


def contract_last(left, right):
    return lax.dot_general(
        left, right, (((1,), (1,)), ((), ())), preferred_element_type=jnp.float32
    )


def exchange(block, axis, bit):
    count = lax.axis_size(axis)
    return lax.ppermute(block, axis, [(i, i ^ bit) for i in range(count)])


def first_sequences(tokens, gap_mask):
    half = jnp.stack([tokens, gap_mask]).astype(jnp.bfloat16)[None]
    bit = lax.axis_size("row") // 4
    while bit >= 1:
        half = jnp.concatenate([half, exchange(half, "row", bit)])
        bit //= 2
    return half


def prepare_kernel(embedding_ref, filters_ref, table_ref, second_ref, letter_s):
    letters, channels = embedding_ref.shape
    kinds = letter_s.shape[0]
    f32, bf16 = jnp.float32, jnp.bfloat16
    letter_s[...] = jnp.zeros_like(letter_s)
    letter_s[0:letters, :] = embedding_ref[...]
    letter = letter_s[...]
    for tap in range(3):
        mixed = LOG2E * lax.dot_general(
            filters_ref[0, tap], letter, (((1,), (1,)), ((), ())),
            precision=lax.Precision.HIGHEST, preferred_element_type=f32,
        )
        plain = jnp.zeros((channels, kinds), f32)
        if tap == 1:
            mixed = mixed + SHIFT
            plain = LOG2E * letter.T - SHIFT
        for first, value in ((0, mixed), (channels, plain)):
            high = value.astype(bf16)
            low = (value - high.astype(f32)).astype(bf16)
            for part, piece in enumerate((high, low)):
                start = (part * 3 + tap) * kinds
                table_ref[first : first + channels, start : start + kinds] = piece
        second_ref[:, tap * channels : (tap + 1) * channels] = filters_ref[1, tap].astype(bf16)


def prepare(embedding, filters):
    letters, channels = embedding.shape
    kinds = -(-letters // 32) * 32
    bf16 = jnp.bfloat16
    return pl.pallas_call(
        prepare_kernel,
        out_shape=[
            jax.ShapeDtypeStruct((2 * channels, 6 * kinds), bf16),
            jax.ShapeDtypeStruct((channels, 3 * channels), bf16),
        ],
        scratch_shapes=[
            pltpu.VMEM((kinds, channels), jnp.float32),
        ],
        compiler_params=pltpu.CompilerParams(vmem_limit_bytes=16 << 20),
        cost_estimate=pl.CostEstimate(flops=10**6, bytes_accessed=1 << 18, transcendentals=0),
    )(in_hbm(embedding), in_hbm(filters))


def feature_kernel(
    dilations, here_ref, there_ref, table_ref, second_ref, row_ref, col_ref, row_mark_ref, col_mark_ref,
    token_s, mark_s, onehot_s, hidden_s, narrow_s, turn_s, stage_s, sems, *, pitch,
):
    first_spread, second_spread = dilations[0], dilations[1]
    blocks, _, each, length = here_ref.shape
    part = blocks * each
    width = 2 * part
    channels = second_ref.shape[0]
    kinds = onehot_s.shape[1]
    rows, cols = row_ref.shape[0], col_ref.shape[1]
    row_first, col_first = lax.axis_index("row") * rows, lax.axis_index("col") * cols
    lanes = LANES
    for side, ref in enumerate((here_ref, there_ref)):
        at = slice(side * part, (side + 1) * part)
        token_s[HALO : HALO + length, at] = ref[:, 0].reshape(part, length).astype(jnp.float32).T
        mark_s[:, at] = ref[:, 1].reshape(part, length).astype(jnp.float32).T
    edge = jnp.full((HALO, width), -1.0, jnp.float32)
    token_s[0:HALO, :] = edge
    token_s[HALO + length : 2 * HALO + length, :] = edge
    row_mark_ref[...] = mark_s[pl.ds(pl.multiple_of(row_first, 8), rows), :].astype(row_mark_ref.dtype)
    col_mark_ref[...] = mark_s[pl.ds(pl.multiple_of(col_first, 8), cols), :].astype(col_mark_ref.dtype)
    letters = lax.broadcasted_iota(jnp.int32, (kinds, width), 0).astype(jnp.float32).astype(onehot_s.dtype)
    present, absent = jnp.ones((), onehot_s.dtype), jnp.zeros((), onehot_s.dtype)
    table = table_ref[...]
    second = second_ref[...]

    def layer_one(at):
        taps = jnp.concatenate([onehot_s[at - first_spread], onehot_s[at], onehot_s[at + first_spread]], axis=0)
        mixing = jnp.dot(table, jnp.concatenate([taps, taps], axis=0), preferred_element_type=jnp.float32)
        shifted = mixing[:channels]
        hidden = mixing[channels:] + jnp.maximum(shifted, jnp.exp2(jnp.minimum(shifted, SHIFT)) + (SHIFT - LOG2E))
        hidden_s[at] = hidden
        narrow_s[at] = hidden.astype(narrow_s.dtype)

    def layer_two(at):
        taps = jnp.concatenate([narrow_s[at - second_spread], narrow_s[at], narrow_s[at + second_spread]], axis=0)
        mixing = jnp.dot(second, taps, preferred_element_type=jnp.float32)
        return hidden_s[at] + jnp.maximum(mixing, LOG2E * jnp.exp2(jnp.minimum(mixing, 0.0)) - LOG2E)

    def run(first, count, emit, before, between, after):
        block = min(BLOCK, count)

        def hot(step, carry):
            block = token_s[pl.ds(pl.multiple_of(first + step * 8, 8), 8), :]
            for k in range(8):
                letter = jnp.broadcast_to(block[k : k + 1, :], (kinds, width)).astype(onehot_s.dtype)
                onehot_s[step * 8 + k] = jnp.where(letter == letters, present, absent)
            return carry

        lax.fori_loop(0, (count + 2 * HALO) // 8, hot, 0)

        def clear(start):
            for k in range(DMAX):
                place = first - HALO + start + k

                @pl.when((place < 0) | (place >= length))
                def _():
                    narrow_s[start + k] = jnp.zeros((channels, width), narrow_s.dtype)

        ahead = block + 2 * DMAX
        for k in range(ahead):
            layer_one(DMAX + k)
        clear(DMAX)

        def trip(step, carry):
            before(step)
            between(step)
            for k in range(block):
                emit(step, k, layer_two(HALO + step * block + k))
            for k in range(block):
                layer_one(DMAX + ahead + step * block + k)
            after(step)
            return carry

        last = count // block - 1
        lax.fori_loop(0, last, trip, 0)
        clear(count + HALO)
        before(last)
        between(last)
        for k in range(block):
            emit(last, k, layer_two(HALO + last * block + k))
        after(last)

    def emit_row(step, k, value):
        index = step * min(BLOCK, rows) + k
        marks = mark_s[pl.ds(row_first + index, 1), :]
        row_ref[index] = (value * marks).astype(row_ref.dtype)

    def emit_col(step, k, value):
        for piece in range(width // lanes):
            turn_s[pl.ds(piece * channels * pitch + k, channels, stride=pitch), :] = value[
                :, piece * lanes : (piece + 1) * lanes
            ]

    def leave(step):
        slot = lax.rem(step, 2)
        start = pl.multiple_of(step * BLOCK, BLOCK)
        return pltpu.make_async_copy(stage_s.at[slot], col_ref.at[:, pl.ds(start, BLOCK), :], sems.at[slot])

    def await_stage(step):
        @pl.when(step >= 3)
        def _():
            leave(step - 3).wait()

    def turn_block(step):
        slot = lax.rem(step + 1, 2)
        start = pl.multiple_of(jnp.maximum(step - 1, 0) * BLOCK, BLOCK)
        marks = mark_s[pl.ds(pl.multiple_of(col_first + start, 8), BLOCK), :]
        for channel in range(channels):
            for piece in range(width // lanes):
                part = slice(piece * lanes, (piece + 1) * lanes)
                place = (piece * channels + channel) * pitch
                stage_s[slot, channel, :, part] = (turn_s[place : place + BLOCK, :] * marks[:, part]).astype(stage_s.dtype)

    def send_block(step):
        @pl.when(step >= 1)
        def _():
            leave(step - 1).start()

    nothing = lambda step: None
    run(row_first, rows, emit_row, nothing, nothing, nothing)
    run(col_first, cols, emit_col, await_stage, turn_block, send_block)
    steps = cols // BLOCK
    if steps >= 3:
        leave(steps - 3).wait()
    turn_block(steps)
    leave(steps - 1).start()
    for step in range(max(steps - 2, 0), steps):
        leave(step).wait()


def features(dilations, here, there, table, second, rows, cols):
    blocks, _, each, length = here.shape
    width = 2 * blocks * each
    channels = second.shape[0]
    kinds = table.shape[1] // 6
    span = max(rows, cols) + 2 * HALO
    pitch = BLOCK + 1
    bf16, f32 = jnp.bfloat16, jnp.float32
    full = lambda shape: pl.BlockSpec(shape, functools.partial(lambda rank, g, s: (0,) * rank, len(shape)))
    return pl.pallas_call(
        functools.partial(feature_kernel, pitch=pitch),
        grid_spec=pltpu.PrefetchScalarGridSpec(
            num_scalar_prefetch=1,
            grid=(1,),
            in_specs=[full(x.shape) for x in (here, there, table, second)],
            out_specs=[
                full((rows, channels, width)),
                pl.BlockSpec(memory_space=pl.ANY),
                full((rows, width)),
                full((cols, width)),
            ],
            scratch_shapes=[
                pltpu.VMEM((length + 2 * HALO, width), f32),
                pltpu.VMEM((length, width), f32),
                pltpu.VMEM((span, kinds, width), bf16),
                pltpu.VMEM((span, channels, width), f32),
                pltpu.VMEM((span, channels, width), bf16),
                pltpu.VMEM((width // 128 * channels * pitch, 128), f32),
                pltpu.VMEM((2, channels, BLOCK, width), bf16),
                pltpu.SemaphoreType.DMA((2,)),
            ],
        ),
        out_shape=[
            jax.ShapeDtypeStruct((rows, channels, width), bf16),
            jax.ShapeDtypeStruct((channels, cols, width), bf16),
            jax.ShapeDtypeStruct((rows, width), bf16),
            jax.ShapeDtypeStruct((cols, width), bf16),
        ],
        compiler_params=pltpu.CompilerParams(vmem_limit_bytes=40 << 20),
        cost_estimate=pl.CostEstimate(
            flops=40 * channels * channels * width * (rows + cols),
            bytes_accessed=2 * channels * width * (rows + cols),
            transcendentals=2 * channels * width * (rows + cols),
        ),
    )(dilations, here, there, table, second)


def outer_kernel(*refs, picks, halves, swap):
    count = len(picks)
    row_refs = refs[: halves * count]
    col_refs = refs[halves * count : halves * (count + 1)]
    projection_ref = refs[halves * (count + 1)]
    marks = refs[halves * (count + 1) + 1 : -(count + 3)]
    pair_refs = refs[-(count + 3) : -3]
    edge_ref, sum_s, turn_s = refs[-3:]
    step = pl.program_id(0)
    group, cols, _ = col_refs[0].shape
    channels = row_refs[0].shape[1]
    rows = count * HALO

    @pl.when(step == 0)
    def _():
        sum_s[...] = jnp.zeros_like(sum_s)

    right = jnp.concatenate([ref[...].reshape(group * cols, ref.shape[2]) for ref in col_refs], axis=1)
    left = jnp.concatenate(
        [
            jnp.concatenate([row_refs[p * halves + h][...].reshape(HALO * channels, -1) for h in range(halves)], axis=1)
            for p in range(count)
        ],
        axis=0,
    )
    pitch = turn_s.shape[0] // channels
    for a in range(channels):
        turn_s[a * pitch : a * pitch + group, :] = projection_ref[a].astype(jnp.float32)
    turned = []
    for b in range(0, group, 2):
        pair = jnp.concatenate([turn_s[pl.ds(b + k, channels, stride=pitch), :] for k in range(2)], axis=0)
        turned.append(pair.T.astype(jnp.bfloat16))
    projection = jnp.concatenate(turned, axis=1)
    outer = contract_last(left, right).astype(jnp.bfloat16)
    for pair in range(0, rows, 2):
        sides = [
            jnp.concatenate(
                [outer[i * channels : (i + 1) * channels, b * cols : (b + 1) * cols] for b in range(group)], axis=0
            )
            for i in (pair, pair + 1)
        ]
        sum_s[pair // 2] += jnp.dot(
            projection, jnp.concatenate(sides, axis=1), preferred_element_type=jnp.float32
        )

    @pl.when(step == pl.num_programs(0) - 1)
    def _():
        row_marks, col_marks = marks[:halves], marks[halves:]
        counts = sum(contract_last(r[...], c[...]) for r, c in zip(row_marks, col_marks))
        share = 1.0 / ((counts + 1.0) * (LOG2E * LOG2E))
        for p, pick in enumerate(picks):
            for k in range(HALO):
                i = p * HALO + k
                place = pick * HALO + k
                value = sum_s[i // 2][:, (i % 2) * cols : (i % 2 + 1) * cols] * share[place : place + 1, :]
                value = value.T
                pair_refs[p][k] = value.astype(edge_ref.dtype)
                if swap:
                    edge_ref[i] = jnp.where(lax.axis_index("col") == 0, value[cols - HALO :], value[:HALO]).astype(edge_ref.dtype)
        if not swap:
            edge_ref[...] = jnp.zeros_like(edge_ref)


def outer_products(row_feats, col_feats, projection, row_marks, col_marks, picks, swap, group=8):
    _, channels, _ = row_feats[0].shape
    cols = col_feats[0].shape[1]
    out = projection.shape[2]
    total = sum(x.shape[2] for x in row_feats)
    tall = len(picks) * HALO
    full = lambda shape: pl.BlockSpec(shape, functools.partial(lambda rank, g: (0,) * rank, len(shape)))
    picked = lambda pick, width: pl.BlockSpec((HALO, channels, width), lambda g: (pick, 0, 0))
    results = pl.pallas_call(
        functools.partial(outer_kernel, picks=picks, halves=len(row_feats), swap=swap),
        grid_spec=pl.GridSpec(
            grid=(channels // group,),
            in_specs=[picked(pick, x.shape[2]) for pick in picks for x in row_feats]
            + [pl.BlockSpec((group, cols, x.shape[2]), lambda g: (g, 0, 0)) for x in col_feats]
            + [pl.BlockSpec((channels, group, out), lambda g: (0, g, 0))]
            + [full(x.shape) for x in (*row_marks, *col_marks)],
            out_specs=[full((HALO, cols, out)) for _ in picks] + [full((tall, HALO, out))],
            scratch_shapes=[
                pltpu.VMEM((tall // 2, out, 2 * cols), jnp.float32),
                pltpu.VMEM((channels * (group + 1), out), jnp.float32),
            ],
        ),
        out_shape=[jax.ShapeDtypeStruct((HALO, cols, out), jnp.bfloat16) for _ in picks]
        + [jax.ShapeDtypeStruct((tall, HALO, out), jnp.bfloat16)],
        compiler_params=pltpu.CompilerParams(vmem_limit_bytes=32 << 20),
        cost_estimate=pl.CostEstimate(
            flops=2 * tall * cols * channels * channels * (total + out),
            bytes_accessed=2 * channels * total * (tall + cols),
            transcendentals=0,
        ),
    )(
        *[x for _ in picks for x in row_feats],
        *col_feats,
        projection,
        *row_marks,
        *col_marks,
    )
    return list(results[:-1]), results[-1]


def conv_kernel(dilations, *refs, length, swap, rows, cols):
    first_spread, second_spread = dilations[NL1], dilations[NL1 + 1]
    row_first, col_first = lax.axis_index("row") * rows, lax.axis_index("col") * cols
    blocks = rows // HALO + 2
    row_refs = refs[:blocks]
    margin_refs = refs[blocks:-9]
    filter_ref, out_ref, wide_s, first_s, hidden_s, second_s, weight_s, out_s, sem = refs[-9:]
    channels = out_ref.shape[2]
    tall, pitch = rows + 2 * DMAX, cols + 2 * HALO
    f32, bf16 = jnp.float32, jnp.bfloat16
    for block, ref in enumerate(row_refs):
        for k in range(HALO):
            start = (block * HALO + k) * pitch + HALO
            wide_s[start : start + cols, :] = ref[k].astype(f32)
    for i in range(rows + 2 * HALO):
        if swap:
            edge = margin_refs[0][i].astype(f32)
            left = jnp.where(col_first == 0, jnp.zeros_like(edge), edge)
            right = jnp.where(col_first == 0, edge, jnp.zeros_like(edge))
        else:
            left, right = margin_refs[0][i].astype(f32), margin_refs[1][i].astype(f32)
        wide_s[i * pitch : i * pitch + HALO, :] = left
        wide_s[i * pitch + HALO + cols : (i + 1) * pitch, :] = right
    for layer in range(2):
        deep = 3 * channels
        weight_s[layer, 3 * deep :, 0:channels] = jnp.zeros((deep, channels), bf16)
        weight_s[layer, :deep, channels:] = jnp.zeros((deep, channels), bf16)
        weight_s[layer, : 3 * deep, 0:channels] = filter_ref[layer]
        weight_s[layer, deep:, channels:] = filter_ref[layer]

    def spread_taps(source, target, count, spread, width, span):
        def body(i, carry):
            for tap in range(3):
                start = i * pitch + DMAX + (tap - 1) * spread
                for at in range(0, width, 16):
                    piece = source[pl.ds(start + at, 16), :].astype(bf16)
                    target[pl.ds(pl.multiple_of(i * span + at, 16), 16), tap * channels : (tap + 1) * channels] = piece
            return carry

        lax.fori_loop(0, count, body, 0, unroll=2)

    for target, count, span in ((first_s, rows + 2 * HALO, pitch), (second_s, tall, cols)):
        target[count * span : (count + DMAX) * span, :] = jnp.zeros((DMAX * span, 3 * channels), bf16)

    def mix(source, layer, pair, spread, span):
        first = 2 * spread * lax.div(pair, spread) + lax.rem(pair, spread)
        taps = jnp.concatenate(
            [
                source[pl.ds(pl.multiple_of((first + DMAX + (tap - 1) * spread) * span, 16), span), :]
                for tap in range(4)
            ],
            axis=1,
        )
        mixing = jnp.dot(taps, weight_s[layer], preferred_element_type=f32)
        return (first, mixing[:, :channels]), (first + spread, mixing[:, channels:])

    spread_taps(wide_s, first_s, rows + 2 * HALO, first_spread, pitch, pitch)

    def one(pair, carry):
        for i, mixing in mix(first_s, 0, pair, first_spread, pitch):
            hidden_s[pl.ds(pl.multiple_of(i * pitch, 8), pitch), :] = elu(mixing)
        return carry

    lax.fori_loop(0, row_pairs(tall), one, 0, unroll=3)
    for i in range(tall):
        place = row_first - DMAX + i
        if i < DMAX or i >= tall - DMAX:

            @pl.when((place < 0) | (place >= length))
            def _():
                hidden_s[i * pitch : (i + 1) * pitch, :] = jnp.zeros((pitch, channels), f32)

    @pl.when(col_first == 0)
    def _():
        for i in range(tall):
            hidden_s[i * pitch : i * pitch + DMAX, :] = jnp.zeros((DMAX, channels), f32)

    @pl.when(col_first + cols == length)
    def _():
        for i in range(tall):
            start = i * pitch + DMAX + cols
            hidden_s[start : start + DMAX, :] = jnp.zeros((DMAX, channels), f32)

    spread_taps(hidden_s, second_s, tall, second_spread, cols, cols)

    def two(pair, carry):
        for i, mixing in mix(second_s, 1, pair, second_spread, cols):
            own = wide_s[pl.ds(pl.multiple_of(jnp.minimum(i + HALO, rows + 2 * HALO - 1) * pitch + HALO, 8), cols), :]
            out_s[i] = (own + mixing).astype(out_s.dtype)
        return carry

    lax.fori_loop(0, row_pairs(rows), two, 0, unroll=3)
    copy = pltpu.make_async_copy(out_s.at[0:rows], out_ref, sem)
    copy.start()
    copy.wait()


def row_pairs(count):
    return max(d * -(-count // (2 * d)) for d in range(1, DMAX + 1))


def pair_convolutions(dilations, blocks, margins, filters, length, swap):
    cols, channels = blocks[0].shape[1:]
    rows = (len(blocks) - 2) * HALO
    pitch = cols + 2 * HALO
    tall = rows + 2 * DMAX
    operands = (*blocks, *margins, filters)
    full = lambda shape: pl.BlockSpec(shape, functools.partial(lambda rank, g, s: (0,) * rank, len(shape)))
    return pl.pallas_call(
        functools.partial(conv_kernel, length=length, swap=swap, rows=rows, cols=cols),
        grid_spec=pltpu.PrefetchScalarGridSpec(
            num_scalar_prefetch=1,
            grid=(1,),
            in_specs=[full(x.shape) for x in operands],
            out_specs=pl.BlockSpec(memory_space=pl.ANY),
            scratch_shapes=[
                pltpu.VMEM(((rows + 2 * HALO) * pitch + HALO, channels), jnp.float32),
                pltpu.VMEM(((tall + 4 * DMAX) * pitch, 3 * channels), jnp.bfloat16),
                pltpu.VMEM(((tall + 2 * DMAX) * pitch, channels), jnp.float32),
                pltpu.VMEM(((rows + 4 * DMAX) * cols, 3 * channels), jnp.bfloat16),
                pltpu.VMEM((2, 12 * channels, 2 * channels), jnp.bfloat16),
                pltpu.VMEM((rows + 2 * DMAX, cols, channels), jnp.bfloat16),
                pltpu.SemaphoreType.DMA,
            ],
        ),
        out_shape=jax.ShapeDtypeStruct((rows, cols, channels), jnp.bfloat16),
        compiler_params=pltpu.CompilerParams(vmem_limit_bytes=40 << 20),
    )(dilations, *operands)


def col_margins(tall):
    steps = range(lax.axis_size("col") - 1)
    head, tail = tall[:, :HALO], tall[:, tall.shape[1] - HALO :]
    return (
        lax.ppermute(tail, "col", [(i, i + 1) for i in steps]),
        lax.ppermute(head, "col", [(i + 1, i) for i in steps]),
    )


def per_device(tokens, gap_mask, dilations, embedding, residue_filters, projection, pair_filters):
    length = tokens.shape[1]
    row_count, col_count = lax.axis_size("row"), lax.axis_size("col")
    rows, cols = length // row_count, length // col_count
    col_index = lax.axis_index("col")
    swap = col_count == 2
    near = first_sequences(tokens, gap_mask)
    near_there = exchange(near, "col", 1)
    far = exchange(near, "row", row_count // 2)
    far_there = exchange(near_there, "row", row_count // 2)
    table, second = prepare(embedding, residue_filters)
    channels = embedding.shape[1]
    blocks = projection.reshape(channels, channels, projection.shape[1])
    near_parts = features(dilations, near, near_there, table, second, rows, cols)
    far_parts = features(dilations, far, far_there, table, second, rows, cols)
    row_feats, col_feats, row_marks, col_marks = zip(near_parts, far_parts)
    last = rows // HALO - 1
    run = functools.partial(outer_products, row_feats, col_feats, blocks, row_marks, col_marks, swap=swap)
    ends, end_edges = run(picks=(0, last))
    steps = range(row_count - 1)
    above = lax.ppermute(ends[1], "row", [(i, i + 1) for i in steps])
    below = lax.ppermute(ends[0], "row", [(i + 1, i) for i in steps])
    if last > 1:
        middle, middle_edges = run(picks=tuple(range(1, last)))
    else:
        middle, middle_edges = [], end_edges[:0]
    blocks = [above, ends[0], *middle, ends[1], below]
    if swap:
        pick = lambda block: jnp.where(col_index == 0, block[:, cols - HALO :], block[:, :HALO])
        edges = jnp.concatenate([pick(above), end_edges[:HALO], middle_edges, end_edges[HALO:], pick(below)])
        edges = exchange(edges, "col", 1)
        margins = [edges]
    else:
        margins = col_margins(jnp.concatenate(blocks))
    filters = pair_filters.reshape(2, 9 * pair_filters.shape[3], pair_filters.shape[4])
    return pair_convolutions(dilations, blocks, margins, filters, length, swap)


def solution(mesh):
    in_specs = (
        P(("grp", "row", "col"), None),
        P(("grp", "row", "col"), None),
        P(),
        P(),
        P(),
        P(),
        P(),
    )
    out_specs = P(("grp", "row"), "col", None)
    return jax.shard_map(per_device, mesh=mesh, in_specs=in_specs, out_specs=out_specs, check_vma=False)
```

```python
import functools
import math

import jax
import jax.numpy as jnp
from jax import lax
from jax.experimental import pallas as pl
from jax.experimental.pallas import tpu as pltpu
from jax.sharding import PartitionSpec as P


NL1 = 2
DMAX = 4
HALO = 2 * DMAX
BLOCK = 32
LANES = 128
LOG2E = 1.4426950408889634
SHIFT = math.log2(LOG2E)


def elu(x):
    return jnp.maximum(x, jnp.exp(jnp.minimum(x, 0.0)) - 1.0)


def in_hbm(array):
    return pltpu.with_memory_space_constraint(array, pltpu.HBM)


def contract_last(left, right):
    return lax.dot_general(
        left, right, (((1,), (1,)), ((), ())), preferred_element_type=jnp.float32
    )


def exchange(block, axis, bit):
    count = lax.axis_size(axis)
    return lax.ppermute(block, axis, [(i, i ^ bit) for i in range(count)])


def first_sequences(tokens, gap_mask):
    half = jnp.stack([tokens, gap_mask]).astype(jnp.bfloat16)[None]
    bit = lax.axis_size("row") // 4
    while bit >= 1:
        half = jnp.concatenate([half, exchange(half, "row", bit)])
        bit //= 2
    return half


def prepare_kernel(embedding_ref, filters_ref, table_ref, second_ref, letter_s):
    letters, channels = embedding_ref.shape
    kinds = letter_s.shape[0]
    f32, bf16 = jnp.float32, jnp.bfloat16
    letter_s[...] = jnp.zeros_like(letter_s)
    letter_s[0:letters, :] = embedding_ref[...]
    letter = letter_s[...]
    for tap in range(3):
        mixed = LOG2E * lax.dot_general(
            filters_ref[0, tap], letter, (((1,), (1,)), ((), ())),
            precision=lax.Precision.HIGHEST, preferred_element_type=f32,
        )
        plain = jnp.zeros((channels, kinds), f32)
        if tap == 1:
            mixed = mixed + SHIFT
            plain = LOG2E * letter.T - SHIFT
        for first, value in ((0, mixed), (channels, plain)):
            high = value.astype(bf16)
            low = (value - high.astype(f32)).astype(bf16)
            for part, piece in enumerate((high, low)):
                start = (part * 3 + tap) * kinds
                table_ref[first : first + channels, start : start + kinds] = piece
        second_ref[:, tap * channels : (tap + 1) * channels] = filters_ref[1, tap].astype(bf16)


def prepare(embedding, filters):
    letters, channels = embedding.shape
    kinds = -(-letters // 32) * 32
    bf16 = jnp.bfloat16
    return pl.pallas_call(
        prepare_kernel,
        out_shape=[
            jax.ShapeDtypeStruct((2 * channels, 6 * kinds), bf16),
            jax.ShapeDtypeStruct((channels, 3 * channels), bf16),
        ],
        scratch_shapes=[
            pltpu.VMEM((kinds, channels), jnp.float32),
        ],
        compiler_params=pltpu.CompilerParams(vmem_limit_bytes=16 << 20),
        cost_estimate=pl.CostEstimate(flops=10**6, bytes_accessed=1 << 18, transcendentals=0),
    )(in_hbm(embedding), in_hbm(filters))


def feature_kernel(
    dilations, here_ref, there_ref, table_ref, second_ref, row_ref, col_ref, row_mark_ref, col_mark_ref,
    token_s, mark_s, onehot_s, hidden_s, narrow_s, turn_s, stage_s, sems, *, pitch,
):
    first_spread, second_spread = dilations[0], dilations[1]
    blocks, _, each, length = here_ref.shape
    part = blocks * each
    width = 2 * part
    channels = second_ref.shape[0]
    kinds = onehot_s.shape[1]
    rows, cols = row_ref.shape[0], col_ref.shape[1]
    row_first, col_first = lax.axis_index("row") * rows, lax.axis_index("col") * cols
    lanes = LANES
    for side, ref in enumerate((here_ref, there_ref)):
        at = slice(side * part, (side + 1) * part)
        token_s[HALO : HALO + length, at] = ref[:, 0].reshape(part, length).astype(jnp.float32).T
        mark_s[:, at] = ref[:, 1].reshape(part, length).astype(jnp.float32).T
    edge = jnp.full((HALO, width), -1.0, jnp.float32)
    token_s[0:HALO, :] = edge
    token_s[HALO + length : 2 * HALO + length, :] = edge
    row_mark_ref[...] = mark_s[pl.ds(pl.multiple_of(row_first, 8), rows), :].astype(row_mark_ref.dtype)
    col_mark_ref[...] = mark_s[pl.ds(pl.multiple_of(col_first, 8), cols), :].astype(col_mark_ref.dtype)
    letters = lax.broadcasted_iota(jnp.int32, (kinds, width), 0).astype(jnp.float32).astype(onehot_s.dtype)
    present, absent = jnp.ones((), onehot_s.dtype), jnp.zeros((), onehot_s.dtype)
    table = table_ref[...]
    second = second_ref[...]

    def layer_one(at):
        taps = jnp.concatenate([onehot_s[at - first_spread], onehot_s[at], onehot_s[at + first_spread]], axis=0)
        mixing = jnp.dot(table, jnp.concatenate([taps, taps], axis=0), preferred_element_type=jnp.float32)
        shifted = mixing[:channels]
        hidden = mixing[channels:] + jnp.maximum(shifted, jnp.exp2(jnp.minimum(shifted, SHIFT)) + (SHIFT - LOG2E))
        hidden_s[at] = hidden
        narrow_s[at] = hidden.astype(narrow_s.dtype)

    def layer_two(at):
        taps = jnp.concatenate([narrow_s[at - second_spread], narrow_s[at], narrow_s[at + second_spread]], axis=0)
        mixing = jnp.dot(second, taps, preferred_element_type=jnp.float32)
        return hidden_s[at] + jnp.maximum(mixing, LOG2E * jnp.exp2(jnp.minimum(mixing, 0.0)) - LOG2E)

    def run(first, count, emit, before, between, after):
        block = min(BLOCK, count)

        def hot(step, carry):
            block = token_s[pl.ds(pl.multiple_of(first + step * 8, 8), 8), :]
            for k in range(8):
                letter = jnp.broadcast_to(block[k : k + 1, :], (kinds, width)).astype(onehot_s.dtype)
                onehot_s[step * 8 + k] = jnp.where(letter == letters, present, absent)
            return carry

        lax.fori_loop(0, (count + 2 * HALO) // 8, hot, 0)

        def clear(start):
            for k in range(DMAX):
                place = first - HALO + start + k

                @pl.when((place < 0) | (place >= length))
                def _():
                    narrow_s[start + k] = jnp.zeros((channels, width), narrow_s.dtype)

        ahead = block + 2 * DMAX
        for k in range(ahead):
            layer_one(DMAX + k)
        clear(DMAX)

        def trip(step, carry):
            before(step)
            between(step)
            for k in range(block):
                emit(step, k, layer_two(HALO + step * block + k))
            for k in range(block):
                layer_one(DMAX + ahead + step * block + k)
            after(step)
            return carry

        last = count // block - 1
        lax.fori_loop(0, last, trip, 0)
        clear(count + HALO)
        before(last)
        between(last)
        for k in range(block):
            emit(last, k, layer_two(HALO + last * block + k))
        after(last)

    def emit_row(step, k, value):
        index = step * min(BLOCK, rows) + k
        marks = mark_s[pl.ds(row_first + index, 1), :]
        row_ref[index] = (value * marks).astype(row_ref.dtype)

    def emit_col(step, k, value):
        for piece in range(width // lanes):
            turn_s[pl.ds(piece * channels * pitch + k, channels, stride=pitch), :] = value[
                :, piece * lanes : (piece + 1) * lanes
            ]

    def leave(step):
        slot = lax.rem(step, 2)
        start = pl.multiple_of(step * BLOCK, BLOCK)
        return pltpu.make_async_copy(stage_s.at[slot], col_ref.at[:, pl.ds(start, BLOCK), :], sems.at[slot])

    def await_stage(step):
        @pl.when(step >= 3)
        def _():
            leave(step - 3).wait()

    def turn_block(step):
        slot = lax.rem(step + 1, 2)
        start = pl.multiple_of(jnp.maximum(step - 1, 0) * BLOCK, BLOCK)
        marks = mark_s[pl.ds(pl.multiple_of(col_first + start, 8), BLOCK), :]
        for channel in range(channels):
            for piece in range(width // lanes):
                part = slice(piece * lanes, (piece + 1) * lanes)
                place = (piece * channels + channel) * pitch
                stage_s[slot, channel, :, part] = (turn_s[place : place + BLOCK, :] * marks[:, part]).astype(stage_s.dtype)

    def send_block(step):
        @pl.when(step >= 1)
        def _():
            leave(step - 1).start()

    nothing = lambda step: None
    run(row_first, rows, emit_row, nothing, nothing, nothing)
    run(col_first, cols, emit_col, await_stage, turn_block, send_block)
    steps = cols // BLOCK
    if steps >= 3:
        leave(steps - 3).wait()
    turn_block(steps)
    leave(steps - 1).start()
    for step in range(max(steps - 2, 0), steps):
        leave(step).wait()


def features(dilations, here, there, table, second, rows, cols):
    blocks, _, each, length = here.shape
    width = 2 * blocks * each
    channels = second.shape[0]
    kinds = table.shape[1] // 6
    span = max(rows, cols) + 2 * HALO
    pitch = BLOCK + 1
    bf16, f32 = jnp.bfloat16, jnp.float32
    full = lambda shape: pl.BlockSpec(shape, functools.partial(lambda rank, g, s: (0,) * rank, len(shape)))
    return pl.pallas_call(
        functools.partial(feature_kernel, pitch=pitch),
        grid_spec=pltpu.PrefetchScalarGridSpec(
            num_scalar_prefetch=1,
            grid=(1,),
            in_specs=[full(x.shape) for x in (here, there, table, second)],
            out_specs=[
                full((rows, channels, width)),
                pl.BlockSpec(memory_space=pl.ANY),
                full((rows, width)),
                full((cols, width)),
            ],
            scratch_shapes=[
                pltpu.VMEM((length + 2 * HALO, width), f32),
                pltpu.VMEM((length, width), f32),
                pltpu.VMEM((span, kinds, width), bf16),
                pltpu.VMEM((span, channels, width), f32),
                pltpu.VMEM((span, channels, width), bf16),
                pltpu.VMEM((width // 128 * channels * pitch, 128), f32),
                pltpu.VMEM((2, channels, BLOCK, width), bf16),
                pltpu.SemaphoreType.DMA((2,)),
            ],
        ),
        out_shape=[
            jax.ShapeDtypeStruct((rows, channels, width), bf16),
            jax.ShapeDtypeStruct((channels, cols, width), bf16),
            jax.ShapeDtypeStruct((rows, width), bf16),
            jax.ShapeDtypeStruct((cols, width), bf16),
        ],
        compiler_params=pltpu.CompilerParams(vmem_limit_bytes=40 << 20),
        cost_estimate=pl.CostEstimate(
            flops=40 * channels * channels * width * (rows + cols),
            bytes_accessed=2 * channels * width * (rows + cols),
            transcendentals=2 * channels * width * (rows + cols),
        ),
    )(dilations, here, there, table, second)


def outer_kernel(*refs, picks, halves, swap):
    count = len(picks)
    row_refs = refs[: halves * count]
    col_refs = refs[halves * count : halves * (count + 1)]
    projection_ref = refs[halves * (count + 1)]
    marks = refs[halves * (count + 1) + 1 : -(count + 3)]
    pair_refs = refs[-(count + 3) : -3]
    edge_ref, sum_s, turn_s = refs[-3:]
    step = pl.program_id(0)
    group, cols, _ = col_refs[0].shape
    channels = row_refs[0].shape[1]
    rows = count * HALO

    @pl.when(step == 0)
    def _():
        sum_s[...] = jnp.zeros_like(sum_s)

    right = jnp.concatenate([ref[...].reshape(group * cols, ref.shape[2]) for ref in col_refs], axis=1)
    left = jnp.concatenate(
        [
            jnp.concatenate([row_refs[p * halves + h][...].reshape(HALO * channels, -1) for h in range(halves)], axis=1)
            for p in range(count)
        ],
        axis=0,
    )
    pitch = turn_s.shape[0] // channels
    for a in range(channels):
        turn_s[a * pitch : a * pitch + group, :] = projection_ref[a].astype(jnp.float32)
    turned = []
    for b in range(0, group, 2):
        pair = jnp.concatenate([turn_s[pl.ds(b + k, channels, stride=pitch), :] for k in range(2)], axis=0)
        turned.append(pair.T.astype(jnp.bfloat16))
    projection = jnp.concatenate(turned, axis=1)
    outer = contract_last(left, right).astype(jnp.bfloat16)
    for pair in range(0, rows, 2):
        sides = [
            jnp.concatenate(
                [outer[i * channels : (i + 1) * channels, b * cols : (b + 1) * cols] for b in range(group)], axis=0
            )
            for i in (pair, pair + 1)
        ]
        sum_s[pair // 2] += jnp.dot(
            projection, jnp.concatenate(sides, axis=1), preferred_element_type=jnp.float32
        )

    @pl.when(step == pl.num_programs(0) - 1)
    def _():
        row_marks, col_marks = marks[:halves], marks[halves:]
        counts = sum(contract_last(r[...], c[...]) for r, c in zip(row_marks, col_marks))
        share = 1.0 / ((counts + 1.0) * (LOG2E * LOG2E))
        for p, pick in enumerate(picks):
            for k in range(HALO):
                i = p * HALO + k
                place = pick * HALO + k
                value = sum_s[i // 2][:, (i % 2) * cols : (i % 2 + 1) * cols] * share[place : place + 1, :]
                value = value.T
                pair_refs[p][k] = value.astype(edge_ref.dtype)
                if swap:
                    edge_ref[i] = jnp.where(lax.axis_index("col") == 0, value[cols - HALO :], value[:HALO]).astype(edge_ref.dtype)
        if not swap:
            edge_ref[...] = jnp.zeros_like(edge_ref)


def outer_products(row_feats, col_feats, projection, row_marks, col_marks, picks, swap, group=8):
    _, channels, _ = row_feats[0].shape
    cols = col_feats[0].shape[1]
    out = projection.shape[2]
    total = sum(x.shape[2] for x in row_feats)
    tall = len(picks) * HALO
    full = lambda shape: pl.BlockSpec(shape, functools.partial(lambda rank, g: (0,) * rank, len(shape)))
    picked = lambda pick, width: pl.BlockSpec((HALO, channels, width), lambda g: (pick, 0, 0))
    results = pl.pallas_call(
        functools.partial(outer_kernel, picks=picks, halves=len(row_feats), swap=swap),
        grid_spec=pl.GridSpec(
            grid=(channels // group,),
            in_specs=[picked(pick, x.shape[2]) for pick in picks for x in row_feats]
            + [pl.BlockSpec((group, cols, x.shape[2]), lambda g: (g, 0, 0)) for x in col_feats]
            + [pl.BlockSpec((channels, group, out), lambda g: (0, g, 0))]
            + [full(x.shape) for x in (*row_marks, *col_marks)],
            out_specs=[full((HALO, cols, out)) for _ in picks] + [full((tall, HALO, out))],
            scratch_shapes=[
                pltpu.VMEM((tall // 2, out, 2 * cols), jnp.float32),
                pltpu.VMEM((channels * (group + 1), out), jnp.float32),
            ],
        ),
        out_shape=[jax.ShapeDtypeStruct((HALO, cols, out), jnp.bfloat16) for _ in picks]
        + [jax.ShapeDtypeStruct((tall, HALO, out), jnp.bfloat16)],
        compiler_params=pltpu.CompilerParams(vmem_limit_bytes=32 << 20),
        cost_estimate=pl.CostEstimate(
            flops=2 * tall * cols * channels * channels * (total + out),
            bytes_accessed=2 * channels * total * (tall + cols),
            transcendentals=0,
        ),
    )(
        *[x for _ in picks for x in row_feats],
        *col_feats,
        projection,
        *row_marks,
        *col_marks,
    )
    return list(results[:-1]), results[-1]


def conv_kernel(dilations, *refs, length, swap, rows, cols):
    first_spread, second_spread = dilations[NL1], dilations[NL1 + 1]
    row_first, col_first = lax.axis_index("row") * rows, lax.axis_index("col") * cols
    blocks = rows // HALO + 2
    row_refs = refs[:blocks]
    margin_refs = refs[blocks:-9]
    filter_ref, out_ref, wide_s, first_s, hidden_s, second_s, weight_s, out_s, sem = refs[-9:]
    channels = out_ref.shape[2]
    tall, pitch = rows + 2 * DMAX, cols + 2 * HALO
    f32, bf16 = jnp.float32, jnp.bfloat16
    for block, ref in enumerate(row_refs):
        for k in range(HALO):
            start = (block * HALO + k) * pitch + HALO
            wide_s[start : start + cols, :] = ref[k].astype(f32)
    for i in range(rows + 2 * HALO):
        if swap:
            edge = margin_refs[0][i].astype(f32)
            left = jnp.where(col_first == 0, jnp.zeros_like(edge), edge)
            right = jnp.where(col_first == 0, edge, jnp.zeros_like(edge))
        else:
            left, right = margin_refs[0][i].astype(f32), margin_refs[1][i].astype(f32)
        wide_s[i * pitch : i * pitch + HALO, :] = left
        wide_s[i * pitch + HALO + cols : (i + 1) * pitch, :] = right
    for layer in range(2):
        deep = 3 * channels
        weight_s[layer, 3 * deep :, 0:channels] = jnp.zeros((deep, channels), bf16)
        weight_s[layer, :deep, channels:] = jnp.zeros((deep, channels), bf16)
        weight_s[layer, : 3 * deep, 0:channels] = filter_ref[layer]
        weight_s[layer, deep:, channels:] = filter_ref[layer]

    def spread_taps(source, target, count, spread, width, span):
        def body(i, carry):
            for tap in range(3):
                start = i * pitch + DMAX + (tap - 1) * spread
                for at in range(0, width, 16):
                    piece = source[pl.ds(start + at, 16), :].astype(bf16)
                    target[pl.ds(pl.multiple_of(i * span + at, 16), 16), tap * channels : (tap + 1) * channels] = piece
            return carry

        lax.fori_loop(0, count, body, 0, unroll=2)

    for target, count, span in ((first_s, rows + 2 * HALO, pitch), (second_s, tall, cols)):
        target[count * span : (count + DMAX) * span, :] = jnp.zeros((DMAX * span, 3 * channels), bf16)

    def mix(source, layer, pair, spread, span):
        first = 2 * spread * lax.div(pair, spread) + lax.rem(pair, spread)
        taps = jnp.concatenate(
            [
                source[pl.ds(pl.multiple_of((first + DMAX + (tap - 1) * spread) * span, 16), span), :]
                for tap in range(4)
            ],
            axis=1,
        )
        mixing = jnp.dot(taps, weight_s[layer], preferred_element_type=f32)
        return (first, mixing[:, :channels]), (first + spread, mixing[:, channels:])

    spread_taps(wide_s, first_s, rows + 2 * HALO, first_spread, pitch, pitch)

    def one(pair, carry):
        for i, mixing in mix(first_s, 0, pair, first_spread, pitch):
            hidden_s[pl.ds(pl.multiple_of(i * pitch, 8), pitch), :] = elu(mixing)
        return carry

    lax.fori_loop(0, row_pairs(tall), one, 0, unroll=at_once(row_pairs(tall)))
    for i in range(tall):
        place = row_first - DMAX + i
        if i < DMAX or i >= tall - DMAX:

            @pl.when((place < 0) | (place >= length))
            def _():
                hidden_s[i * pitch : (i + 1) * pitch, :] = jnp.zeros((pitch, channels), f32)

    @pl.when(col_first == 0)
    def _():
        for i in range(tall):
            hidden_s[i * pitch : i * pitch + DMAX, :] = jnp.zeros((DMAX, channels), f32)

    @pl.when(col_first + cols == length)
    def _():
        for i in range(tall):
            start = i * pitch + DMAX + cols
            hidden_s[start : start + DMAX, :] = jnp.zeros((DMAX, channels), f32)

    spread_taps(hidden_s, second_s, tall, second_spread, cols, cols)

    def two(pair, carry):
        for i, mixing in mix(second_s, 1, pair, second_spread, cols):
            own = wide_s[pl.ds(pl.multiple_of(jnp.minimum(i + HALO, rows + 2 * HALO - 1) * pitch + HALO, 8), cols), :]
            out_s[i] = (own + mixing).astype(out_s.dtype)
        return carry

    lax.fori_loop(0, row_pairs(rows), two, 0, unroll=at_once(row_pairs(rows)))
    copy = pltpu.make_async_copy(out_s.at[0:rows], out_ref, sem)
    copy.start()
    copy.wait()


def at_once(count):
    return max(k for k in range(1, 8) if count % k == 0)


def row_pairs(count):
    return max(d * -(-count // (2 * d)) for d in range(1, DMAX + 1))


def pair_convolutions(dilations, blocks, margins, filters, length, swap):
    cols, channels = blocks[0].shape[1:]
    rows = (len(blocks) - 2) * HALO
    pitch = cols + 2 * HALO
    tall = rows + 2 * DMAX
    operands = (*blocks, *margins, filters)
    full = lambda shape: pl.BlockSpec(shape, functools.partial(lambda rank, g, s: (0,) * rank, len(shape)))
    return pl.pallas_call(
        functools.partial(conv_kernel, length=length, swap=swap, rows=rows, cols=cols),
        grid_spec=pltpu.PrefetchScalarGridSpec(
            num_scalar_prefetch=1,
            grid=(1,),
            in_specs=[full(x.shape) for x in operands],
            out_specs=pl.BlockSpec(memory_space=pl.ANY),
            scratch_shapes=[
                pltpu.VMEM(((rows + 2 * HALO) * pitch + HALO, channels), jnp.float32),
                pltpu.VMEM(((tall + 4 * DMAX) * pitch, 3 * channels), jnp.bfloat16),
                pltpu.VMEM(((tall + 2 * DMAX) * pitch, channels), jnp.float32),
                pltpu.VMEM(((rows + 4 * DMAX) * cols, 3 * channels), jnp.bfloat16),
                pltpu.VMEM((2, 12 * channels, 2 * channels), jnp.bfloat16),
                pltpu.VMEM((rows + 2 * DMAX, cols, channels), jnp.bfloat16),
                pltpu.SemaphoreType.DMA,
            ],
        ),
        out_shape=jax.ShapeDtypeStruct((rows, cols, channels), jnp.bfloat16),
        compiler_params=pltpu.CompilerParams(vmem_limit_bytes=40 << 20),
    )(dilations, *operands)


def col_margins(tall):
    steps = range(lax.axis_size("col") - 1)
    head, tail = tall[:, :HALO], tall[:, tall.shape[1] - HALO :]
    return (
        lax.ppermute(tail, "col", [(i, i + 1) for i in steps]),
        lax.ppermute(head, "col", [(i + 1, i) for i in steps]),
    )


def per_device(tokens, gap_mask, dilations, embedding, residue_filters, projection, pair_filters):
    length = tokens.shape[1]
    row_count, col_count = lax.axis_size("row"), lax.axis_size("col")
    rows, cols = length // row_count, length // col_count
    col_index = lax.axis_index("col")
    swap = col_count == 2
    near = first_sequences(tokens, gap_mask)
    near_there = exchange(near, "col", 1)
    far = exchange(near, "row", row_count // 2)
    far_there = exchange(near_there, "row", row_count // 2)
    table, second = prepare(embedding, residue_filters)
    channels = embedding.shape[1]
    blocks = projection.reshape(channels, channels, projection.shape[1])
    near_parts = features(dilations, near, near_there, table, second, rows, cols)
    far_parts = features(dilations, far, far_there, table, second, rows, cols)
    row_feats, col_feats, row_marks, col_marks = zip(near_parts, far_parts)
    last = rows // HALO - 1
    run = functools.partial(outer_products, row_feats, col_feats, blocks, row_marks, col_marks, swap=swap)
    ends, end_edges = run(picks=(0, last))
    steps = range(row_count - 1)
    above = lax.ppermute(ends[1], "row", [(i, i + 1) for i in steps])
    below = lax.ppermute(ends[0], "row", [(i + 1, i) for i in steps])
    if last > 1:
        middle, middle_edges = run(picks=tuple(range(1, last)))
    else:
        middle, middle_edges = [], end_edges[:0]
    blocks = [above, ends[0], *middle, ends[1], below]
    if swap:
        pick = lambda block: jnp.where(col_index == 0, block[:, cols - HALO :], block[:, :HALO])
        edges = jnp.concatenate([pick(above), end_edges[:HALO], middle_edges, end_edges[HALO:], pick(below)])
        edges = exchange(edges, "col", 1)
        margins = [edges]
    else:
        margins = col_margins(jnp.concatenate(blocks))
    filters = pair_filters.reshape(2, 9 * pair_filters.shape[3], pair_filters.shape[4])
    return pair_convolutions(dilations, blocks, margins, filters, length, swap)


def solution(mesh):
    in_specs = (
        P(("grp", "row", "col"), None),
        P(("grp", "row", "col"), None),
        P(),
        P(),
        P(),
        P(),
        P(),
    )
    out_specs = P(("grp", "row"), "col", None)
    return jax.shard_map(per_device, mesh=mesh, in_specs=in_specs, out_specs=out_specs, check_vma=False)
```
